128 devices in a mesh: ctx: 64 (over z, y, x), ch: 2 (over core).
Axes of the slice: x: 4, y: 4, z: 4, core: 2. Of those that a mesh axis runs over, the one named last changes fastest.
Arguments:
- conv_input: bfloat16 [16384, 8192], P(('ctx', 'ch')), may hold values from -6 to 6
- gate_branch: bfloat16 [16384, 8192], P(('ctx', 'ch')), may hold values from -6 to 6
- out_grad: bfloat16 [16384, 8192], P(('ctx', 'ch')), may hold values from -6 to 6
- short_filter: bfloat16 [7, 8192], P(None, 'ch'), may hold values from -2 to 2
- medium_filter: bfloat16 [128, 512], P(None, 'ch'), may hold values from -0.5 to 0.5
- decay_rates: float32 [512, 16], P('ch'), may hold values from 1.2207031e-05 to 0.125
- residues: float32 [512, 16], P('ch'), may hold values from -0.45 to 0.45
- direct_term: float32 [8192], P('ch'), may hold values from -3 to 3
Outputs:
- input_grad: bfloat16 [16384, 8192], P(('ctx', 'ch'))
- gate_grad: bfloat16 [16384, 8192], P(('ctx', 'ch'))
The draws below stay inside these ranges and needn't reach their ends.
All inputs are finite; a program needn't handle non-finite values.
Results may differ from the reference program's by a relative error of at most 0.015.
Values may be sent and summed in bfloat16 or wider, within the bound.
A program may use at most 192 MiB of HBM per device.

```python
import math
import jax
import jax.numpy as jnp
import numpy as np
from jax import lax

D = 8192
GSIZE = 16
POLES = 16
KS = 7
KM = 128
TOK_DEV = 256
GROUPS = 512
SEQ = 16384


def band_layout(slow_count, middle_count, quick_count):
    bands = [(math.log(0.2 / SEQ), math.log(2.0 / SEQ), slow_count, 0.3), (math.log(0.1 / TOK_DEV), math.log(4.0 / TOK_DEV), middle_count, 0.6), (math.log(4.0 / TOK_DEV), math.log(0.125), quick_count, 0.3)]
    lowest, highest, weights = ([], [], [])
    for low_end, high_end, amount, weight_value in bands:
        for stratum in range(amount):
            lowest.append(low_end + (high_end - low_end) * stratum / amount)
            highest.append(low_end + (high_end - low_end) * (stratum + 1) / amount)
            weights.append(weight_value)
    return (np.array(lowest, np.float32), np.array(highest, np.float32), np.array(weights, np.float32))


def shuffle_one(single_key):
    return jax.random.permutation(single_key, POLES)


def decay_law(key):
    base = jax.random.fold_in(key, 11)
    slow_count = 5 * POLES // 16
    quick_count = 3 * POLES // 16
    lowest, highest, weights = band_layout(slow_count, POLES - slow_count - quick_count, quick_count)
    jitter = jax.random.uniform(jax.random.fold_in(base, 1), (GROUPS, POLES), jnp.float32)
    log_rates = jnp.asarray(lowest)[None, :] + jnp.asarray(highest - lowest)[None, :] * jitter
    orders = jax.vmap(shuffle_one)(jax.random.split(jax.random.fold_in(base, 2), GROUPS))
    rates = jnp.take_along_axis(jnp.exp(log_rates), orders, axis=1)
    factors = jnp.take_along_axis(jnp.broadcast_to(jnp.asarray(weights)[None, :], (GROUPS, POLES)), orders, axis=1)
    return (jnp.clip(rates, 0.2 / float(SEQ), 0.125), factors)


def draw_decay_rates(key, part):
    rates, factors = decay_law(key)
    return rates


def draw_residues(key, part):
    rates, factors = decay_law(key)
    noise = jnp.clip(jax.random.normal(jax.random.fold_in(key, 22), (GROUPS, POLES), jnp.float32), -3.0, 3.0)
    return jnp.clip(noise * jnp.sqrt(2.0 * rates) * factors, -0.45, 0.45)


def block_levels(own_key, shape, cuts, low, high):
    gain = 1.0
    for dim, shards_of in cuts:
        steps = jax.random.uniform(jax.random.fold_in(jax.random.fold_in(own_key, 6), dim), (shards_of,), jnp.float32, low / len(cuts), high / len(cuts))
        gain = gain * jnp.repeat(jnp.exp(steps), shape[dim] // shards_of).reshape((-1,) + (1,) * (len(shape) - 1 - dim))
    return gain


def scatter_about(stream_key, extent, spread, bound, cuts=(), kind=jnp.bfloat16):
    values = spread * jax.random.normal(stream_key, extent, jnp.float32)
    if cuts:
        values = values * block_levels(stream_key, extent, cuts, -0.22, 0.18)
    return jnp.clip(values, -bound, bound).astype(kind)


def setup_inputs(seed: int = 0) -> dict:
    splits = jax.random.split(jax.random.key(seed), 9)
    conv_input = scatter_about(splits[0], (SEQ, D), 1.0, 6.0, ((0, 128),))
    gate_branch = scatter_about(splits[1], (SEQ, D), 1.0, 6.0, ((0, 128),))
    out_grad = scatter_about(splits[2], (SEQ, D), 1.0, 6.0, ((0, 128),))
    short_filter = scatter_about(splits[3], (KS, D), KS ** -0.5, 2.0, ((1, 2),))
    medium_filter = scatter_about(splits[4], (KM, GROUPS), KM ** -0.5, 0.5, ((1, 2),))
    decay_rates = draw_decay_rates(jax.random.fold_in(splits[8], 71), 0)
    residues = draw_residues(jax.random.fold_in(splits[8], 71), 0)
    direct_term = scatter_about(splits[7], (D,), 0.5, 3.0, ((0, 2),), jnp.float32)
    return {"conv_input": conv_input, "gate_branch": gate_branch, "out_grad": out_grad, "short_filter": short_filter, "medium_filter": medium_filter, "decay_rates": decay_rates, "residues": residues, "direct_term": direct_term}


def slice_work(items):
    signal, grad_y, out_grad, short_part, medium_part, rate_part, residue_part, direct_part = items
    length_all, slice_width = signal.shape
    poles = rate_part.shape[1]
    decay = jnp.repeat(jnp.exp(-rate_part), GSIZE, axis=0).T
    weight = jnp.repeat(residue_part, GSIZE, axis=0).T

    def advance(state, row):
        state = decay * state + row[None, :]
        return state, jnp.sum(weight * state, axis=0)

    empty_state = jnp.zeros((poles, slice_width), jnp.float32)
    forward_in = signal.astype(jnp.float32)
    _, causal = lax.scan(advance, empty_state, forward_in)
    conv_out = lax.optimization_barrier((direct_part[None, :] * forward_in + causal).astype(jnp.bfloat16))
    gate_grad = (out_grad.astype(jnp.float32) * conv_out.astype(jnp.float32)).astype(jnp.bfloat16)
    backward_in = grad_y.astype(jnp.float32)
    _, anticausal = lax.scan(advance, empty_state, backward_in, reverse=True)
    grad_b = (direct_part[None, :] * backward_in + anticausal).astype(jnp.bfloat16)
    med_taps = medium_part.shape[0]
    tap_table = jnp.repeat(medium_part.astype(jnp.float32), GSIZE, axis=1)
    padded = jnp.concatenate([grad_b, jnp.zeros((med_taps, slice_width), jnp.bfloat16)]).astype(jnp.float32)

    def add_tap(index, total):
        index = index.astype(jnp.int32)
        factor = lax.dynamic_slice_in_dim(tap_table, index, 1, 0)
        return total + factor * lax.dynamic_slice_in_dim(padded, index, length_all, 0)

    grad_a = lax.fori_loop(0, med_taps, add_tap, jnp.zeros((length_all, slice_width), jnp.float32))
    grad_a = lax.optimization_barrier(grad_a.astype(jnp.bfloat16))
    padded_a = jnp.concatenate([grad_a, jnp.zeros((8, slice_width), jnp.bfloat16)]).astype(jnp.float32)
    result = jnp.zeros((length_all, slice_width), jnp.float32)
    for offset in range(short_part.shape[0]):
        result = result + short_part[offset].astype(jnp.float32)[None, :] * padded_a[offset:offset + length_all]
    return result.astype(jnp.bfloat16), gate_grad


def split_channels(array, slices):
    return array.reshape(array.shape[0], slices, array.shape[1] // slices).transpose(1, 0, 2)


def join_channels(array):
    return array.transpose(1, 0, 2).reshape(array.shape[1], array.shape[0] * array.shape[2])


def reference(conv_input, gate_branch, out_grad, short_filter, medium_filter, decay_rates, residues, direct_term):
    slices = 8
    grad_y = (out_grad.astype(jnp.float32) * gate_branch.astype(jnp.float32)).astype(jnp.bfloat16)
    grad_y = lax.optimization_barrier(grad_y)
    items = (split_channels(conv_input, slices), split_channels(grad_y, slices), split_channels(out_grad, slices),
             split_channels(short_filter, slices), split_channels(medium_filter, slices),
             decay_rates.reshape(slices, decay_rates.shape[0] // slices, decay_rates.shape[1]),
             residues.reshape(slices, residues.shape[0] // slices, residues.shape[1]),
             direct_term.reshape(slices, direct_term.shape[0] // slices))
    input_parts, gate_parts = lax.map(slice_work, items)
    return join_channels(input_parts), join_channels(gate_parts)
```

```python
import functools

import jax
import jax.numpy as jnp
from jax import lax
from jax.experimental import pallas as pl
from jax.experimental.pallas import tpu as pltpu
from jax.sharding import PartitionSpec as P

MESH = pl.DeviceIdType.MESH
F32 = jnp.float32
BF16 = jnp.bfloat16
L = 128
G = 8
SPLIT = 4
UNROLL = 4


def iota(shape, dim):
    return lax.broadcasted_iota(jnp.int32, shape, dim)


def matmul(a, b):
    return lax.dot_general(a, b, (((1,), (0,)), ((), ())), preferred_element_type=F32)


def column(row):
    return jnp.broadcast_to(row, (L, L)).T


def own_groups(block):
    shape = block.shape
    keep = (iota(shape, 0) // 16) == ((iota(shape, 1) % L) // 16)
    return jnp.sum(jnp.where(keep, block, 0.0).reshape(G, 16, shape[1]), axis=0)


def spread_groups(states):
    shape = (L, states.shape[1])
    keep = (iota(shape, 0) // 16) == ((iota(shape, 1) % L) // 16)
    return jnp.where(keep, jnp.concatenate([states] * G, axis=0), 0.0)


def masked_stack(data):
    lanes = (iota((1, data.shape[1]), 1) % L) // 16
    return jnp.concatenate([data * (lanes == g).astype(F32).astype(BF16) for g in range(G)], axis=0)


def circulant(row):
    return pltpu.roll(jnp.broadcast_to(row, (L, L)), 0, 1, stride=1, stride_axis=0)


def kernel(
    x, gate, og, rate_in, weight_in, direct_in, short_in, medium_in, grad_out, gate_out,
    rate, weight, direct, short, medium, flipped, grad_y, taps, rate_lanes, sums, near, conv, adj, halo,
    buf_c, send_x, buf_x, send_y, buf_y, send_z, buf_z, push_y, buf_w, push_x, buf_r, push_c, states,
    head, head_next, tail, rows, ends,
    sem_p, sem_l, sem_n, sem_c, sem_x, sem_y, sem_z, sem_w, sem_r, sem_d, sem_h, sem_e,
):
    channels = x.shape[1]
    blocks = channels // L
    half, quarter, eighth = channels // 2, channels // 8, channels // 32
    ctx, c = lax.axis_index("ctx"), lax.axis_index("ch")
    px, py, pz = ctx % 4, (ctx // 4) % 4, ctx // 16
    me = ctx * 2 + c
    before_me, after_me = (me + 127) % 128, (me + 1) % 128
    last = me == 127

    def at(z_, y_, x_):
        return (z_ * 16 + y_ * 4 + x_, c)

    partner = (ctx, 1 - c)
    previous = (before_me // 2, before_me % 2)
    following = (after_me // 2, after_me % 2)
    mates_x = [at(pz, py, (px + d) % 4) for d in (1, 2, 3)]
    mates_y = [at(pz, (py + d) % 4, px) for d in (1, 2, 3)]
    mates_z = [at((pz + d) % 4, py, px) for d in (1, 2, 3)]
    barrier = pltpu.get_barrier_semaphore()
    for mate in [partner, following] + mates_x + mates_y + mates_z:
        pl.semaphore_signal(barrier, inc=1, device_id=mate, device_id_type=MESH)
    pl.semaphore_wait(barrier, 11)

    def push(src, dst, sem, k, mate):
        copy = pltpu.make_async_remote_copy(
            src, dst, sem.at[0, k], sem.at[1, k], device_id=mate, device_id_type=MESH
        )
        copy.start()
        return copy

    def lanes_of(start, size):
        return pl.ds(pl.multiple_of(start, L), size)

    copies = []
    for k, (own, full) in enumerate(
        [(rate_in, rate), (weight_in, weight), (direct_in, direct), (medium_in, medium)]
    ):
        count = own.shape[0]
        place = full.at[pl.ds(pl.multiple_of(c * count, 8), count), :]
        copies.append(push(own, place, sem_p, k, partner))
        here = pltpu.make_async_copy(own, place, sem_l.at[k])
        here.start()
        copies.append(here)
    mine, theirs = lanes_of(c * half, half), lanes_of((1 - c) * half, half)
    copies.append(push(short_in, short.at[:, mine], sem_p, 4, partner))
    here = pltpu.make_async_copy(short_in, short.at[:, mine], sem_l.at[4])
    here.start()
    copies.append(here)
    for copy in copies:
        copy.wait()

    lane, sub = iota((L, L), 1), iota((L, L), 0)
    flip = (lane + sub == 127).astype(F32).astype(BF16)

    def over_blocks(body, start, stop):
        def step(i, _):
            for u in range(UNROLL):
                body(i * UNROLL + u, u)
            return 0

        lax.fori_loop(start // UNROLL, stop // UNROLL, step, 0)

    def block_sums(b, u):
        cols = lanes_of(b * L, L)
        rate_col, weight_col = column(rate[pl.ds(b, 1), :]), column(weight[pl.ds(b, 1), :])
        decay = jnp.exp(-rate_col * lane.astype(F32))
        taps[pl.ds(pl.multiple_of(b * G, G), G), :] = jnp.sum((weight_col * decay).reshape(G, 16, L), axis=1)
        y = (og[:, cols].astype(F32) * gate[:, cols].astype(F32)).astype(BF16)
        back = matmul(flip, x[:, cols]).astype(BF16)
        grad_y[:, cols] = y
        flipped[:, cols] = back
        both = own_groups(matmul(decay.astype(BF16), jnp.concatenate([back, y], axis=1)))
        sums[0, :, cols] = both[:, :L].astype(BF16)
        sums[1, :, cols] = both[:, L:].astype(BF16)
        rate_lanes[:, cols] = own_groups(rate_col)

    def local_products(b, u):
        cols = lanes_of(b * L, L)
        k = taps[pl.ds(pl.multiple_of(b * G, G), G), :]
        table = [jnp.where(lane >= sub, circulant(k[g : g + 1, :]), 0.0).astype(BF16) for g in range(G)]
        y = grad_y[:, cols]
        data = jnp.concatenate([flipped[:, cols], y], axis=1)
        both = matmul(jnp.concatenate(table, axis=1), masked_stack(data))
        conv[:, cols] = both[:, :L].astype(BF16)
        adj[:, cols] = (both[:, L:] + direct[pl.ds(b, 1), :] * y.astype(F32)).astype(BF16)

    halo_copies = []

    def local_piece(k):
        size = blocks // SPLIT
        over_blocks(local_products, k * size, (k + 1) * size)
        cols = slice(k * size * L, (k + 1) * size * L)
        halo_copies.append(push(adj.at[:, cols], halo.at[:, cols], sem_h, k, previous))

    over_blocks(block_sums, 0, blocks)
    near_copy = push(sums.at[1], near, sem_n, 0, previous)
    fore_copy = push(sums.at[0, :, theirs], buf_c.at[0], sem_c, 0, partner)
    local_piece(0)
    near_copy.wait()

    near[...] = jnp.where(last, 0.0, near[...].astype(F32)).astype(BF16)
    back_copy = push(near.at[:, theirs], buf_c.at[1], sem_c, 1, partner)
    step = jnp.exp(-rate_lanes[:, mine] * 128.0)

    def ordered(own, other):
        return jnp.where(c == 0, own, other), jnp.where(c == 0, other, own)

    fore_copy.wait()
    first_a, second_a = ordered(sums[0, :, mine].astype(F32), buf_c[0].astype(F32))
    send_x[0] = (second_a + step * first_a).astype(BF16)
    back_copy.wait()
    first_b, second_b = ordered(near[:, mine].astype(F32), buf_c[1].astype(F32))
    send_x[1] = (first_b + step * second_b).astype(BF16)

    def power(rate_, span, count):
        return jnp.exp(-rate_ * (float(span) * jnp.maximum(count, 0).astype(F32)))

    def total(buf, span, rate_):
        p1 = jnp.exp(-rate_ * float(span))
        sum_a, sum_b = buf[0, 0].astype(F32), buf[3, 1].astype(F32)
        for j in (1, 2, 3):
            sum_a = sum_a * p1 + buf[j, 0].astype(F32)
            sum_b = sum_b * p1 + buf[3 - j, 1].astype(F32)
        return sum_a, sum_b

    def exclusive(buf, span, place, rate_, before, after):
        sum_a = before * power(rate_, span, place)
        sum_b = after * power(rate_, span, 3 - place)
        for j in range(4):
            sum_a += (j < place).astype(F32) * power(rate_, span, place - 1 - j) * buf[j, 0].astype(F32)
            sum_b += (j > place).astype(F32) * power(rate_, span, j - 1 - place) * buf[j, 1].astype(F32)
        return sum_a, sum_b

    def put(ref, pair):
        ref[0], ref[1] = pair[0].astype(BF16), pair[1].astype(BF16)

    copies = []
    for k, d in enumerate((1, 2, 3)):
        piece = send_x.at[:, :, lanes_of(((px + d) % 4) * quarter, quarter)]
        copies.append(push(piece, buf_x.at[px], sem_x, k, mates_x[k]))
    buf_x[px] = send_x[:, :, lanes_of(px * quarter, quarter)]
    rate_x = rate_lanes[:, lanes_of(c * half + px * quarter, quarter)]
    rate_y = rate_lanes[:, lanes_of(c * half + px * quarter + py * eighth, eighth)]
    local_piece(1)
    for copy in copies:
        copy.wait()
    put(send_y, total(buf_x, 256, rate_x))
    copies = []
    for k, d in enumerate((1, 2, 3)):
        piece = send_y.at[:, :, lanes_of(((py + d) % 4) * eighth, eighth)]
        copies.append(push(piece, buf_y.at[py], sem_y, k, mates_y[k]))
    buf_y[py] = send_y[:, :, lanes_of(py * eighth, eighth)]
    local_piece(2)
    for copy in copies:
        copy.wait()
    put(send_z, total(buf_y, 1024, rate_y))
    copies = [push(send_z, buf_z.at[pz], sem_z, k, mates_z[k]) for k in range(3)]
    buf_z[pz] = send_z[...]
    local_piece(3)
    for copy in copies:
        copy.wait()
    zero = jnp.zeros_like(rate_y)
    before, after = exclusive(buf_z, 4096, pz, rate_y, zero, zero)
    copies = []
    for k, d in enumerate((1, 2, 3)):
        put(push_y.at[k], exclusive(buf_y, 1024, (py + d) % 4, rate_y, before, after))
        copies.append(push(push_y.at[k], buf_w.at[py], sem_w, k, mates_y[k]))
    put(buf_w.at[py], exclusive(buf_y, 1024, py, rate_y, before, after))
    for copy in copies:
        copy.wait()
    before = jnp.concatenate([buf_w[j, 0] for j in range(4)], axis=1).astype(F32)
    after = jnp.concatenate([buf_w[j, 1] for j in range(4)], axis=1).astype(F32)
    copies = []
    for k, d in enumerate((1, 2, 3)):
        put(push_x.at[k], exclusive(buf_x, 256, (px + d) % 4, rate_x, before, after))
        copies.append(push(push_x.at[k], buf_r.at[px], sem_r, k, mates_x[k]))
    put(buf_r.at[px], exclusive(buf_x, 256, px, rate_x, before, after))
    for copy in copies:
        copy.wait()
    for j in range(4):
        lanes = pl.ds(j * quarter, quarter)
        part = slice(j * quarter, (j + 1) * quarter)
        early_a, late_b = buf_r[j, 0].astype(F32), buf_r[j, 1].astype(F32)
        late_a = first_a[:, part] + step[:, part] * early_a
        early_b = second_b[:, part] + step[:, part] * late_b
        push_c[0, :, lanes] = jnp.where(c == 0, late_a, early_a).astype(BF16)
        push_c[1, :, lanes] = jnp.where(c == 0, late_b, early_b).astype(BF16)
        keep = lanes_of(c * half + j * quarter, quarter)
        states[0, :, keep] = jnp.where(c == 0, early_a, late_a).astype(BF16)
        states[1, :, keep] = jnp.where(c == 0, early_b, late_b).astype(BF16)
    push(push_c, states.at[:, :, mine], sem_d, 0, partner).wait()
    for copy in halo_copies:
        copy.wait()

    for u in range(UNROLL):
        rows[u, L : L + 8, :] = jnp.zeros((8, L), F32)

    def adjoint_filters(b, u):
        cols = lanes_of(b * L, L)
        into = (weight[pl.ds(b, 1), :] * jnp.exp(-rate[pl.ds(b, 1), :] * (L - sub).astype(F32))).astype(BF16)
        far = states[1, :, cols].astype(F32)
        close = near[:, cols].astype(F32) + jnp.exp(-rate_lanes[:, cols] * 128.0) * far
        entering = spread_groups(jnp.concatenate([close, far], axis=1)).astype(BF16)
        beyond = jnp.where(last, 0.0, halo[:, cols].astype(F32))
        inside = jnp.concatenate([adj[:, cols].astype(F32), beyond], axis=1)
        grad_b = (inside + matmul(into, entering)).astype(BF16)
        m = medium[pl.ds(pl.multiple_of(b * G, G), G), :]
        now, then = [], []
        for g in range(G):
            table = circulant(m[g : g + 1, :])
            now.append(jnp.where(lane >= sub, table, 0.0).astype(BF16))
            then.append(jnp.where(lane < sub, table, 0.0).astype(BF16))
        tables = jnp.concatenate([jnp.concatenate(now, axis=1), jnp.concatenate(then, axis=1)], axis=0)
        both = matmul(tables, masked_stack(grad_b))
        grad_a = (both[:L, :L] + both[L:, L:]).astype(BF16)
        rows[u, 0:L, :] = grad_a.astype(F32)
        head[:, cols] = rows[u, 0:8, :]
        tail[:, cols] = rows[u, 112:128, :]
        taps_s = short[:, cols]
        sum_k = taps_s[0:1, :] * rows[u, 0:L, :]
        for k in range(1, 7):
            sum_k += taps_s[k : k + 1, :] * rows[u, k : k + L, :]
        grad_out[:, cols] = sum_k.astype(BF16)

    over_blocks(adjoint_filters, 0, blocks)
    head_copy = push(head, head_next, sem_e, 0, previous)

    def gate_gradient(b, u):
        cols = lanes_of(b * L, L)
        into = (weight[pl.ds(b, 1), :] * jnp.exp(-rate[pl.ds(b, 1), :] * (sub + 1).astype(F32))).astype(BF16)
        entering = spread_groups(states[0, :, cols].astype(F32)).astype(BF16)
        full = matmul(jnp.concatenate([flip, into], axis=1), jnp.concatenate([conv[:, cols], entering], axis=0))
        full = (full + direct[pl.ds(b, 1), :] * x[:, cols].astype(F32)).astype(BF16)
        gate_out[:, cols] = (og[:, cols].astype(F32) * full.astype(F32)).astype(BF16)

    over_blocks(gate_gradient, 0, blocks)
    head_copy.wait()

    def last_rows(b, u):
        cols = lanes_of(b * L, L)
        ends[u, 0:16, :] = tail[:, cols]
        ends[u, 16:24, :] = jnp.where(last, 0.0, head_next[:, cols])
        taps_s = short[:, cols]
        sum_k = taps_s[0:1, :] * ends[u, 0:16, :]
        for k in range(1, 7):
            sum_k += taps_s[k : k + 1, :] * ends[u, k : k + 16, :]
        grad_out[112:128, cols] = sum_k.astype(BF16)

    over_blocks(last_rows, 0, blocks)


def on_device(x, gate, og, short_filter, medium_filter, decay_rates, residues, direct_term):
    channels = x.shape[1]
    groups = channels // 16
    rows = decay_rates.shape[0] // G
    half, quarter, eighth = channels // 2, channels // 8, channels // 32
    wide = pltpu.VMEM((L, channels), BF16)
    vmem, dma = pltpu.VMEM, pltpu.SemaphoreType.DMA
    return pl.pallas_call(
        kernel,
        out_shape=(jax.ShapeDtypeStruct(x.shape, BF16),) * 2,
        in_specs=[pl.BlockSpec(memory_space=pltpu.VMEM)] * 8,
        out_specs=(pl.BlockSpec(memory_space=pltpu.VMEM),) * 2,
        scratch_shapes=[
            vmem((2 * rows, L), F32),
            vmem((2 * rows, L), F32),
            vmem((2 * rows, L), F32),
            vmem((8, channels), F32),
            vmem((groups, L), F32),
            wide,
            wide,
            vmem((groups, L), F32),
            vmem((16, channels), F32),
            vmem((2, 16, channels), BF16),
            vmem((16, channels), BF16),
            wide,
            wide,
            wide,
            vmem((2, 16, half), BF16),
            vmem((2, 16, half), BF16),
            vmem((4, 2, 16, quarter), BF16),
            vmem((2, 16, quarter), BF16),
            vmem((4, 2, 16, eighth), BF16),
            vmem((2, 16, eighth), BF16),
            vmem((4, 2, 16, eighth), BF16),
            vmem((3, 2, 16, eighth), BF16),
            vmem((4, 2, 16, eighth), BF16),
            vmem((3, 2, 16, quarter), BF16),
            vmem((4, 2, 16, quarter), BF16),
            vmem((2, 16, half), BF16),
            vmem((2, 16, channels), BF16),
            vmem((8, channels), F32),
            vmem((8, channels), F32),
            vmem((16, channels), F32),
            vmem((UNROLL, L + 8, L), F32),
            vmem((UNROLL, 24, L), F32),
            dma((2, 5)), dma((5,)), dma((2, 1)), dma((2, 2)), dma((2, 3)), dma((2, 3)), dma((2, 3)),
            dma((2, 3)), dma((2, 3)), dma((2, 1)), dma((2, SPLIT)), dma((2, 1)),
        ],
        compiler_params=pltpu.CompilerParams(
            collective_id=0, has_side_effects=True, vmem_limit_bytes=58 * 2**20
        ),
    )(
        x,
        gate,
        og,
        decay_rates.reshape(rows, L),
        residues.reshape(rows, L),
        direct_term.reshape(rows, L),
        jnp.pad(short_filter.astype(F32), ((0, 1), (0, 0))),
        medium_filter.astype(F32).T,
    )


def solution(mesh):
    placed = (
        P(("ctx", "ch"), None),
        P(("ctx", "ch"), None),
        P(("ctx", "ch"), None),
        P(None, "ch"),
        P(None, "ch"),
        P("ch", None),
        P("ch", None),
        P("ch"),
    )
    return jax.shard_map(
        on_device,
        mesh=mesh,
        in_specs=placed,
        out_specs=(P(("ctx", "ch"), None), P(("ctx", "ch"), None)),
        check_vma=False,
    )
```

```python
import functools

import jax
import jax.numpy as jnp
from jax import lax
from jax.experimental import pallas as pl
from jax.experimental.pallas import tpu as pltpu
from jax.sharding import PartitionSpec as P

MESH = pl.DeviceIdType.MESH
F32 = jnp.float32
BF16 = jnp.bfloat16
L = 128
G = 8
SPLIT = 8
UNROLL = 4


def iota(shape, dim):
    return lax.broadcasted_iota(jnp.int32, shape, dim)


def matmul(a, b):
    return lax.dot_general(a, b, (((1,), (0,)), ((), ())), preferred_element_type=F32)


def column(row):
    return jnp.broadcast_to(row, (L, L)).T


def own_groups(block):
    shape = block.shape
    keep = (iota(shape, 0) // 16) == ((iota(shape, 1) % L) // 16)
    return jnp.sum(jnp.where(keep, block, 0.0).reshape(G, 16, shape[1]), axis=0)


def spread_groups(states):
    shape = (L, states.shape[1])
    keep = (iota(shape, 0) // 16) == ((iota(shape, 1) % L) // 16)
    return jnp.where(keep, jnp.concatenate([states] * G, axis=0), 0.0)


def masked_stack(data):
    lanes = (iota((1, data.shape[1]), 1) % L) // 16
    return jnp.concatenate([data * (lanes == g).astype(F32).astype(BF16) for g in range(G)], axis=0)


def circulant(row):
    return pltpu.roll(jnp.broadcast_to(row, (L, L)), 0, 1, stride=1, stride_axis=0)


def kernel(
    x_in, gate_in, og_in, rate_in, weight_in, direct_in, short_in, medium_in, grad_done, gate_done,
    x, gate, og, grad_out, gate_out, rate_by_group, weight_by_group, medium_raw, circ,
    rate, weight, direct, short, medium, flipped, grad_y, taps, rate_lanes, sums, near, conv, adj, halo,
    buf_c, send_x, buf_x, send_y, buf_y, send_z, buf_z, push_y, buf_w, push_x, buf_r, push_c, states,
    head, head_next, tail, rows, ends,
    sem_i, sem_o, sem_p, sem_l, sem_n, sem_c, sem_x, sem_y, sem_z, sem_w, sem_r, sem_d, sem_h, sem_e,
):
    channels = x_in.shape[1]
    blocks = channels // L
    wide = channels // SPLIT
    half, quarter, eighth = channels // 2, channels // 8, channels // 32
    ctx, c = lax.axis_index("ctx"), lax.axis_index("ch")
    px, py, pz = ctx % 4, (ctx // 4) % 4, ctx // 16
    me = ctx * 2 + c
    before_me, after_me = (me + 127) % 128, (me + 1) % 128
    last = me == 127

    def at(z_, y_, x_):
        return (z_ * 16 + y_ * 4 + x_, c)

    partner = (ctx, 1 - c)
    previous = (before_me // 2, before_me % 2)
    following = (after_me // 2, after_me % 2)
    mates_x = [at(pz, py, (px + d) % 4) for d in (1, 2, 3)]
    mates_y = [at(pz, (py + d) % 4, px) for d in (1, 2, 3)]
    mates_z = [at((pz + d) % 4, py, px) for d in (1, 2, 3)]
    loads = []
    for k, (src, dst) in enumerate([(x_in, x), (gate_in, gate), (og_in, og)]):
        loads.append(pltpu.make_async_copy(src, dst, sem_i.at[k]))
        loads[-1].start()
    barrier = pltpu.get_barrier_semaphore()
    for mate in [partner, following] + mates_x + mates_y + mates_z:
        pl.semaphore_signal(barrier, inc=1, device_id=mate, device_id_type=MESH)
    pl.semaphore_wait(barrier, 11)

    def push(src, dst, sem, k, mate):
        copy = pltpu.make_async_remote_copy(
            src, dst, sem.at[0, k], sem.at[1, k], device_id=mate, device_id_type=MESH
        )
        copy.start()
        return copy

    def lanes_of(start, size):
        return pl.ds(pl.multiple_of(start, L), size)

    mine, theirs = lanes_of(c * half, half), lanes_of((1 - c) * half, half)
    count = rate_in.shape[1]
    groups_mine = lanes_of(c * count, count)
    places = [
        (rate_in, rate_by_group.at[:, groups_mine]),
        (weight_in, weight_by_group.at[:, groups_mine]),
        (medium_in, medium_raw.at[:, groups_mine]),
        (direct_in, direct.at[pl.ds(pl.multiple_of(c * direct_in.shape[0], 8), direct_in.shape[0]), :]),
        (short_in, short.at[:, mine]),
    ]
    gathers, here = [], []
    for k, (own, place) in enumerate(places):
        gathers.append(push(own, place, sem_p, k, partner))
        here.append(pltpu.make_async_copy(own, place, sem_l.at[k]))
        here[-1].start()
    for copy in here + loads:
        copy.wait()

    lane, sub = iota((L, L), 1), iota((L, L), 0)
    flip = (lane + sub == 127).astype(F32).astype(BF16)

    def over_blocks(body, start, size):
        def step(i, _):
            for u in range(UNROLL):
                body(start + i * UNROLL + u, u)
            return 0

        lax.fori_loop(0, size // UNROLL, step, 0)

    def block_sums(b, u):
        cols = lanes_of(b * L, L)
        tile = lanes_of((b // 16) * L, L)
        pick = (b % 16) * G + iota((16, L), 1) // 16
        diagonal = iota((16, L), 0) == iota((16, L), 1) % 16
        rate_here = jnp.take_along_axis(rate_by_group[:, tile], pick, axis=1)
        weight_here = jnp.take_along_axis(weight_by_group[:, tile], pick, axis=1)
        rate_row = jnp.sum(jnp.where(diagonal, rate_here, 0.0), axis=0, keepdims=True)
        weight_row = jnp.sum(jnp.where(diagonal, weight_here, 0.0), axis=0, keepdims=True)
        rate_lanes[:, cols] = rate_here
        rate[pl.ds(b, 1), :] = rate_row
        weight[pl.ds(b, 1), :] = weight_row
        rate_col, weight_col = column(rate_row), column(weight_row)
        decay = jnp.exp(-rate_col * lane.astype(F32))
        taps[pl.ds(pl.multiple_of(b * G, G), G), :] = jnp.sum((weight_col * decay).reshape(G, 16, L), axis=1)
        y = (og[:, cols].astype(F32) * gate[:, cols].astype(F32)).astype(BF16)
        back = matmul(flip, x[:, cols]).astype(BF16)
        grad_y[:, cols] = y
        flipped[:, cols] = back
        both = own_groups(matmul(decay.astype(BF16), jnp.concatenate([back, y], axis=1)))
        sums[0, :, cols] = both[:, :L].astype(BF16)
        sums[1, :, cols] = both[:, L:].astype(BF16)

    def local_products(b, u):
        cols = lanes_of(b * L, L)
        k = taps[pl.ds(pl.multiple_of(b * G, G), G), :]
        table = [jnp.where(lane >= sub, circulant(k[g : g + 1, :]), 0.0).astype(BF16) for g in range(G)]
        y = grad_y[:, cols]
        data = jnp.concatenate([flipped[:, cols], y], axis=1)
        both = matmul(jnp.concatenate(table, axis=1), masked_stack(data))
        conv[:, cols] = both[:, :L].astype(BF16)
        adj[:, cols] = (both[:, L:] + direct[pl.ds(b, 1), :] * y.astype(F32)).astype(BF16)

    def medium_tables(b, u):
        m = medium[pl.ds(pl.multiple_of(b * G, G), G), :]
        for g in range(G):
            circ[b, :, g * L : g * L + L] = circulant(m[g : g + 1, :]).astype(BF16)

    size = blocks // SPLIT
    halo_copies = []

    def local_pieces(first, stop):
        over_blocks(local_products, first * size, (stop - first) * size)

    def push_halo(first, stop):
        for k in range(first, stop):
            cols = slice(k * wide, (k + 1) * wide)
            halo_copies.append(push(adj.at[:, cols], halo.at[:, cols], sem_h, k, previous))

    over_blocks(block_sums, c * (blocks // 2), blocks // 2)
    for copy in gathers:
        copy.wait()
    over_blocks(block_sums, (1 - c) * (blocks // 2), blocks // 2)
    near_copy = push(sums.at[1], near, sem_n, 0, previous)
    fore_copy = push(sums.at[0, :, theirs], buf_c.at[0], sem_c, 0, partner)
    for k in range(medium.shape[0] // L):
        medium[k * L : k * L + L, :] = medium_raw[:, k * L : k * L + L].astype(F32).T
    local_pieces(0, 1)
    near_copy.wait()

    near[...] = jnp.where(last, 0.0, near[...].astype(F32)).astype(BF16)
    back_copy = push(near.at[:, theirs], buf_c.at[1], sem_c, 1, partner)
    step = jnp.exp(-rate_lanes[:, mine] * 128.0)

    def ordered(own, other):
        return jnp.where(c == 0, own, other), jnp.where(c == 0, other, own)

    fore_copy.wait()
    first_a, second_a = ordered(sums[0, :, mine].astype(F32), buf_c[0].astype(F32))
    send_x[0] = (second_a + step * first_a).astype(BF16)
    back_copy.wait()
    first_b, second_b = ordered(near[:, mine].astype(F32), buf_c[1].astype(F32))
    send_x[1] = (first_b + step * second_b).astype(BF16)

    def power(rate_, span, count):
        return jnp.exp(-rate_ * (float(span) * jnp.maximum(count, 0).astype(F32)))

    def total(buf, span, rate_):
        p1 = jnp.exp(-rate_ * float(span))
        sum_a, sum_b = buf[0, 0].astype(F32), buf[3, 1].astype(F32)
        for j in (1, 2, 3):
            sum_a = sum_a * p1 + buf[j, 0].astype(F32)
            sum_b = sum_b * p1 + buf[3 - j, 1].astype(F32)
        return sum_a, sum_b

    def exclusive(buf, span, place, rate_, before, after):
        sum_a = before * power(rate_, span, place)
        sum_b = after * power(rate_, span, 3 - place)
        for j in range(4):
            sum_a += (j < place).astype(F32) * power(rate_, span, place - 1 - j) * buf[j, 0].astype(F32)
            sum_b += (j > place).astype(F32) * power(rate_, span, j - 1 - place) * buf[j, 1].astype(F32)
        return sum_a, sum_b

    def put(ref, pair):
        ref[0], ref[1] = pair[0].astype(BF16), pair[1].astype(BF16)

    copies = []
    for k, d in enumerate((1, 2, 3)):
        piece = send_x.at[:, :, lanes_of(((px + d) % 4) * quarter, quarter)]
        copies.append(push(piece, buf_x.at[px], sem_x, k, mates_x[k]))
    buf_x[px] = send_x[:, :, lanes_of(px * quarter, quarter)]
    rate_x = rate_lanes[:, lanes_of(c * half + px * quarter, quarter)]
    rate_y = rate_lanes[:, lanes_of(c * half + px * quarter + py * eighth, eighth)]
    local_pieces(1, 4)
    for copy in copies:
        copy.wait()
    put(send_y, total(buf_x, 256, rate_x))
    copies = []
    for k, d in enumerate((1, 2, 3)):
        piece = send_y.at[:, :, lanes_of(((py + d) % 4) * eighth, eighth)]
        copies.append(push(piece, buf_y.at[py], sem_y, k, mates_y[k]))
    buf_y[py] = send_y[:, :, lanes_of(py * eighth, eighth)]
    push_halo(0, 3)
    local_pieces(4, 6)
    for copy in copies:
        copy.wait()
    put(send_z, total(buf_y, 1024, rate_y))
    copies = [push(send_z, buf_z.at[pz], sem_z, k, mates_z[k]) for k in range(3)]
    buf_z[pz] = send_z[...]
    local_pieces(6, 8)
    for copy in copies:
        copy.wait()
    zero = jnp.zeros_like(rate_y)
    before, after = exclusive(buf_z, 4096, pz, rate_y, zero, zero)
    copies = []
    for k, d in enumerate((1, 2, 3)):
        put(push_y.at[k], exclusive(buf_y, 1024, (py + d) % 4, rate_y, before, after))
        copies.append(push(push_y.at[k], buf_w.at[py], sem_w, k, mates_y[k]))
    put(buf_w.at[py], exclusive(buf_y, 1024, py, rate_y, before, after))
    over_blocks(medium_tables, 0, blocks // 2)
    for copy in copies:
        copy.wait()
    before = jnp.concatenate([buf_w[j, 0] for j in range(4)], axis=1).astype(F32)
    after = jnp.concatenate([buf_w[j, 1] for j in range(4)], axis=1).astype(F32)
    copies = []
    for k, d in enumerate((1, 2, 3)):
        put(push_x.at[k], exclusive(buf_x, 256, (px + d) % 4, rate_x, before, after))
        copies.append(push(push_x.at[k], buf_r.at[px], sem_r, k, mates_x[k]))
    put(buf_r.at[px], exclusive(buf_x, 256, px, rate_x, before, after))
    over_blocks(medium_tables, blocks // 2, blocks // 2)
    for copy in copies:
        copy.wait()
    push_halo(3, SPLIT)
    for j in range(4):
        lanes = pl.ds(j * quarter, quarter)
        part = slice(j * quarter, (j + 1) * quarter)
        early_a, late_b = buf_r[j, 0].astype(F32), buf_r[j, 1].astype(F32)
        late_a = first_a[:, part] + step[:, part] * early_a
        early_b = second_b[:, part] + step[:, part] * late_b
        push_c[0, :, lanes] = jnp.where(c == 0, late_a, early_a).astype(BF16)
        push_c[1, :, lanes] = jnp.where(c == 0, late_b, early_b).astype(BF16)
        keep = lanes_of(c * half + j * quarter, quarter)
        states[0, :, keep] = jnp.where(c == 0, early_a, late_a).astype(BF16)
        states[1, :, keep] = jnp.where(c == 0, early_b, late_b).astype(BF16)
    push(push_c, states.at[:, :, mine], sem_d, 0, partner).wait()

    for u in range(UNROLL):
        rows[u, L : L + 8, :] = jnp.zeros((8, L), F32)

    upper = jnp.concatenate([(lane >= sub).astype(F32).astype(BF16)] * G, axis=1)
    lower = jnp.concatenate([(lane < sub).astype(F32).astype(BF16)] * G, axis=1)

    def adjoint_filters(b, u):
        cols = lanes_of(b * L, L)
        into = (weight[pl.ds(b, 1), :] * jnp.exp(-rate[pl.ds(b, 1), :] * (L - sub).astype(F32))).astype(BF16)
        far = states[1, :, cols].astype(F32)
        close = near[:, cols].astype(F32) + jnp.exp(-rate_lanes[:, cols] * 128.0) * far
        entering = spread_groups(jnp.concatenate([close, far], axis=1)).astype(BF16)
        beyond = jnp.where(last, 0.0, halo[:, cols].astype(F32))
        inside = jnp.concatenate([adj[:, cols].astype(F32), beyond], axis=1)
        grad_b = (inside + matmul(into, entering)).astype(BF16)
        table = circ[b]
        tables = jnp.concatenate([table * upper, table * lower], axis=0)
        both = matmul(tables, masked_stack(grad_b))
        grad_a = (both[:L, :L] + both[L:, L:]).astype(BF16)
        rows[u, 0:L, :] = grad_a.astype(F32)
        head[:, cols] = rows[u, 0:8, :].astype(BF16)
        tail[:, cols] = rows[u, 112:128, :]
        taps_s = short[:, cols].astype(F32)
        sum_k = taps_s[0:1, :] * rows[u, 0:L, :]
        for k in range(1, 7):
            sum_k += taps_s[k : k + 1, :] * rows[u, k : k + L, :]
        grad_out[:, cols] = sum_k.astype(BF16)

    def gate_gradient(b, u):
        cols = lanes_of(b * L, L)
        into = (weight[pl.ds(b, 1), :] * jnp.exp(-rate[pl.ds(b, 1), :] * (sub + 1).astype(F32))).astype(BF16)
        entering = spread_groups(states[0, :, cols].astype(F32)).astype(BF16)
        full = matmul(jnp.concatenate([flip, into], axis=1), jnp.concatenate([conv[:, cols], entering], axis=0))
        full = (full + direct[pl.ds(b, 1), :] * x[:, cols].astype(F32)).astype(BF16)
        gate_out[:, cols] = (og[:, cols].astype(F32) * full.astype(F32)).astype(BF16)

    head_copies, stores = [], []
    for k in range(SPLIT):
        cols = slice(k * wide, (k + 1) * wide)
        halo_copies[k].wait()
        over_blocks(adjoint_filters, k * size, size)
        head_copies.append(push(head.at[:, cols], head_next.at[:, cols], sem_e, k, previous))
        over_blocks(gate_gradient, k * size, size)
        stores.append(pltpu.make_async_copy(gate_out.at[:, cols], gate_done.at[:, cols], sem_o.at[0, k]))
        stores.append(pltpu.make_async_copy(grad_out.at[0:112, cols], grad_done.at[0:112, cols], sem_o.at[1, k]))
        for copy in stores[-2:]:
            copy.start()
    for copy in head_copies:
        copy.wait()

    def last_rows(b, u):
        cols = lanes_of(b * L, L)
        ends[u, 0:16, :] = tail[:, cols]
        ends[u, 16:24, :] = jnp.where(last, 0.0, head_next[:, cols].astype(F32))
        taps_s = short[:, cols].astype(F32)
        sum_k = taps_s[0:1, :] * ends[u, 0:16, :]
        for k in range(1, 7):
            sum_k += taps_s[k : k + 1, :] * ends[u, k : k + 16, :]
        grad_out[112:128, cols] = sum_k.astype(BF16)

    over_blocks(last_rows, 0, blocks)
    stores.append(pltpu.make_async_copy(grad_out.at[112:128, :], grad_done.at[112:128, :], sem_o.at[2, 0]))
    stores[-1].start()
    for copy in stores:
        copy.wait()


def on_device(x, gate, og, short_filter, medium_filter, decay_rates, residues, direct_term):
    channels = x.shape[1]
    groups = channels // 16
    rows = decay_rates.shape[0] // G
    half, quarter, eighth = channels // 2, channels // 8, channels // 32
    wide = pltpu.VMEM((L, channels), BF16)
    vmem, dma = pltpu.VMEM, pltpu.SemaphoreType.DMA
    return pl.pallas_call(
        kernel,
        out_shape=(jax.ShapeDtypeStruct(x.shape, BF16),) * 2,
        in_specs=[pl.BlockSpec(memory_space=pl.ANY)] * 3 + [pl.BlockSpec(memory_space=pltpu.VMEM)] * 5,
        out_specs=(pl.BlockSpec(memory_space=pl.ANY),) * 2,
        scratch_shapes=[
            wide, wide, wide, wide, wide,
            vmem((16, groups), F32),
            vmem((16, groups), F32),
            vmem((L, groups), BF16),
            vmem((channels // L, L, G * L), BF16),
            vmem((2 * rows, L), F32),
            vmem((2 * rows, L), F32),
            vmem((2 * rows, L), F32),
            vmem((7, channels), BF16),
            vmem((groups, L), F32),
            wide,
            wide,
            vmem((groups, L), F32),
            vmem((16, channels), F32),
            vmem((2, 16, channels), BF16),
            vmem((16, channels), BF16),
            wide,
            wide,
            wide,
            vmem((2, 16, half), BF16),
            vmem((2, 16, half), BF16),
            vmem((4, 2, 16, quarter), BF16),
            vmem((2, 16, quarter), BF16),
            vmem((4, 2, 16, eighth), BF16),
            vmem((2, 16, eighth), BF16),
            vmem((4, 2, 16, eighth), BF16),
            vmem((3, 2, 16, eighth), BF16),
            vmem((4, 2, 16, eighth), BF16),
            vmem((3, 2, 16, quarter), BF16),
            vmem((4, 2, 16, quarter), BF16),
            vmem((2, 16, half), BF16),
            vmem((2, 16, channels), BF16),
            vmem((8, channels), BF16),
            vmem((8, channels), BF16),
            vmem((16, channels), F32),
            vmem((UNROLL, L + 8, L), F32),
            vmem((UNROLL, 24, L), F32),
            dma((3,)), dma((3, SPLIT)), dma((2, 5)), dma((5,)), dma((2, 1)), dma((2, 2)), dma((2, 3)), dma((2, 3)), dma((2, 3)),
            dma((2, 3)), dma((2, 3)), dma((2, 1)), dma((2, SPLIT)), dma((2, SPLIT)),
        ],
        compiler_params=pltpu.CompilerParams(
            collective_id=0, has_side_effects=True, vmem_limit_bytes=58 * 2**20
        ),
    )(
        x,
        gate,
        og,
        decay_rates.T,
        residues.T,
        direct_term.reshape(rows, L),
        short_filter,
        medium_filter,
    )


def solution(mesh):
    placed = (
        P(("ctx", "ch"), None),
        P(("ctx", "ch"), None),
        P(("ctx", "ch"), None),
        P(None, "ch"),
        P(None, "ch"),
        P("ch", None),
        P("ch", None),
        P("ch"),
    )
    return jax.shard_map(
        on_device,
        mesh=mesh,
        in_specs=placed,
        out_specs=(P(("ctx", "ch"), None), P(("ctx", "ch"), None)),
        check_vma=False,
    )
```

```python
import functools

import jax
import jax.numpy as jnp
from jax import lax
from jax.experimental import pallas as pl
from jax.experimental.pallas import tpu as pltpu
from jax.sharding import PartitionSpec as P

MESH = pl.DeviceIdType.MESH
F32 = jnp.float32
BF16 = jnp.bfloat16
L = 128
G = 8
SPLIT = 8
UNROLL = 4


def iota(shape, dim):
    return lax.broadcasted_iota(jnp.int32, shape, dim)


def matmul(a, b):
    return lax.dot_general(a, b, (((1,), (0,)), ((), ())), preferred_element_type=F32)


def column(row):
    return jnp.broadcast_to(row, (L, L)).T


def own_groups(block):
    shape = block.shape
    keep = (iota(shape, 0) // 16) == ((iota(shape, 1) % L) // 16)
    return jnp.sum(jnp.where(keep, block, 0.0).reshape(G, 16, shape[1]), axis=0)


def spread_groups(states):
    shape = (L, states.shape[1])
    keep = (iota(shape, 0) // 16) == ((iota(shape, 1) % L) // 16)
    return jnp.where(keep, jnp.concatenate([states] * G, axis=0), 0.0)


def masked_stack(data):
    lanes = (iota((1, data.shape[1]), 1) % L) // 16
    return jnp.concatenate([data * (lanes == g).astype(F32).astype(BF16) for g in range(G)], axis=0)


def circulant(row):
    return pltpu.roll(jnp.broadcast_to(row, (L, L)), 0, 1, stride=1, stride_axis=0)


def kernel(
    x_in, gate_in, og_in, rate_in, weight_in, direct_in, short_in, medium_in, grad_done, gate_done,
    x, gate, og, grad_out, gate_out, rate_by_group, weight_by_group, medium_raw, circ,
    rate, weight, direct, short, medium, grad_y, rate_lanes, sums, near, conv, adj, halo,
    buf_c, send_x, buf_x, send_y, buf_y, send_z, buf_z, push_z, push_y, buf_w, push_x, buf_r, push_c, states,
    head, head_next, tail, rows, ends,
    sem_i, sem_o, sem_p, sem_l, sem_n, sem_c, sem_x, sem_y, sem_z, sem_w, sem_r, sem_d, sem_h, sem_e,
):
    channels = x_in.shape[1]
    blocks = channels // L
    wide = channels // SPLIT
    half, quarter, eighth = channels // 2, channels // 8, channels // 32
    ctx, c = lax.axis_index("ctx"), lax.axis_index("ch")
    px, py, pz = ctx % 4, (ctx // 4) % 4, ctx // 16
    me = ctx * 2 + c
    before_me, after_me = (me + 127) % 128, (me + 1) % 128
    last = me == 127

    def at(z_, y_, x_):
        return (z_ * 16 + y_ * 4 + x_, c)

    partner = (ctx, 1 - c)
    previous = (before_me // 2, before_me % 2)
    following = (after_me // 2, after_me % 2)
    mates_x = [at(pz, py, (px + d) % 4) for d in (1, 2, 3)]
    mates_y = [at(pz, (py + d) % 4, px) for d in (1, 2, 3)]
    mates_z = [at((pz + d) % 4, py, px) for d in (1, 2, 3)]
    loads = []
    for k, (src, dst) in enumerate([(x_in, x), (gate_in, gate), (og_in, og)]):
        loads.append(pltpu.make_async_copy(src, dst, sem_i.at[k]))
        loads[-1].start()
    barrier = pltpu.get_barrier_semaphore()
    for mate in [partner, following] + mates_x + mates_y + mates_z:
        pl.semaphore_signal(barrier, inc=1, device_id=mate, device_id_type=MESH)

    def push(src, dst, sem, k, mate):
        copy = pltpu.make_async_remote_copy(
            src, dst, sem.at[0, k], sem.at[1, k], device_id=mate, device_id_type=MESH
        )
        copy.start()
        return copy

    def lanes_of(start, size):
        return pl.ds(pl.multiple_of(start, L), size)

    mine, theirs = lanes_of(c * half, half), lanes_of((1 - c) * half, half)
    count = rate_in.shape[1]
    groups_mine = lanes_of(c * count, count)
    places = [
        (rate_in, rate_by_group.at[:, groups_mine]),
        (weight_in, weight_by_group.at[:, groups_mine]),
        (medium_in, medium_raw.at[:, groups_mine]),
        (direct_in, direct.at[pl.ds(pl.multiple_of(c * direct_in.shape[0], 8), direct_in.shape[0]), :]),
        (short_in, short.at[:, mine]),
    ]
    here = []
    for k, (own, place) in enumerate(places):
        here.append(pltpu.make_async_copy(own, place, sem_l.at[k]))
        here[-1].start()
    for copy in here + loads:
        copy.wait()

    lane, sub = iota((L, L), 1), iota((L, L), 0)
    flip = (lane + sub == 127).astype(F32).astype(BF16)

    def over_blocks(body, start, size):
        def step(i, _):
            for u in range(UNROLL):
                body(start + i * UNROLL + u, u)
            return 0

        lax.fori_loop(0, size // UNROLL, step, 0)

    def block_sums(b, u):
        cols = lanes_of(b * L, L)
        tile = lanes_of((b // 16) * L, L)
        pick = (b % 16) * G + iota((16, L), 1) // 16
        diagonal = iota((16, L), 0) == iota((16, L), 1) % 16
        rate_here = jnp.take_along_axis(rate_by_group[:, tile], pick, axis=1)
        weight_here = jnp.take_along_axis(weight_by_group[:, tile], pick, axis=1)
        rate_row = jnp.sum(jnp.where(diagonal, rate_here, 0.0), axis=0, keepdims=True)
        weight_row = jnp.sum(jnp.where(diagonal, weight_here, 0.0), axis=0, keepdims=True)
        rate_lanes[:, cols] = rate_here
        rate[pl.ds(b, 1), :] = rate_row
        weight[pl.ds(b, 1), :] = weight_row
        rate_col = column(rate_row)
        ahead = jnp.exp(-rate_col * (127 - lane).astype(F32)).astype(BF16)
        behind = jnp.exp(-rate_col * lane.astype(F32)).astype(BF16)
        y = (og[:, cols].astype(F32) * gate[:, cols].astype(F32)).astype(BF16)
        grad_y[:, cols] = y
        both = matmul(jnp.concatenate([ahead, behind], axis=0), jnp.concatenate([x[:, cols], y], axis=1))
        sums[0, :, cols] = own_groups(both[:L, :L]).astype(BF16)
        sums[1, :, cols] = own_groups(both[L:, L:]).astype(BF16)

    def local_products(b, u):
        cols = lanes_of(b * L, L)
        decay = jnp.exp(-column(rate[pl.ds(b, 1), :]) * lane.astype(F32))
        k = jnp.sum((column(weight[pl.ds(b, 1), :]) * decay).reshape(G, 16, L), axis=1)
        back = matmul(flip, x[:, cols]).astype(BF16)
        table = [jnp.where(lane >= sub, circulant(k[g : g + 1, :]), 0.0).astype(BF16) for g in range(G)]
        y = grad_y[:, cols]
        data = jnp.concatenate([back, y], axis=1)
        both = matmul(jnp.concatenate(table, axis=1), masked_stack(data))
        conv[:, cols] = both[:, :L].astype(BF16)
        adj[:, cols] = (both[:, L:] + direct[pl.ds(b, 1), :] * y.astype(F32)).astype(BF16)

    def medium_tables(b, u):
        m = medium[pl.ds(pl.multiple_of(b * G, G), G), :]
        for g in range(G):
            circ[b, :, g * L : g * L + L] = circulant(m[g : g + 1, :]).astype(BF16)

    size = blocks // SPLIT
    halo_copies = []

    def piece(k, core):
        return (core * (SPLIT // 2) + k) % SPLIT

    def local_pieces(first, stop):
        for k in range(first, stop):
            over_blocks(local_products, piece(k, c) * size, size)

    def push_halo(first, stop):
        for k in range(first, stop):
            cols = lanes_of(piece(k, c) * wide, wide)
            halo_copies.append(push(adj.at[:, cols], halo.at[:, cols], sem_h, k, previous))

    over_blocks(block_sums, c * (blocks // 2), blocks // 2)
    pl.semaphore_wait(barrier, 11)
    gathers = [push(own, place, sem_p, k, partner) for k, (own, place) in enumerate(places)]
    local_pieces(0, 1)
    for copy in gathers:
        copy.wait()
    over_blocks(block_sums, (1 - c) * (blocks // 2), blocks // 2)
    first_copy = push(sums.at[:, :, theirs], buf_c, sem_c, 0, partner)
    for k in range(medium.shape[0] // L):
        medium[k * L : k * L + L, :] = medium_raw[:, k * L : k * L + L].astype(F32).T
    local_pieces(1, 2)

    step = jnp.exp(-rate_lanes[:, mine] * 128.0)
    own = sums[:, :, mine].astype(F32)
    first_copy.wait()
    other = buf_c[...].astype(F32)
    first_a, second_a = jnp.where(c == 0, own[0], other[0]), jnp.where(c == 0, other[0], own[0])
    first_b, second_b = jnp.where(c == 0, own[1], other[1]), jnp.where(c == 0, other[1], own[1])
    send_x[0] = (second_a + step * first_a).astype(BF16)
    send_x[1] = (first_b + step * second_b).astype(BF16)

    def total(buf, span, rate_):
        p1 = jnp.exp(-rate_ * float(span))
        sum_a, sum_b = buf[0, 0].astype(F32), buf[3, 1].astype(F32)
        for j in (1, 2, 3):
            sum_a = sum_a * p1 + buf[j, 0].astype(F32)
            sum_b = sum_b * p1 + buf[3 - j, 1].astype(F32)
        return sum_a, sum_b

    def exclusive(buf, span, rate_, before, after, dst):
        p1 = jnp.exp(-rate_ * float(span))
        for j in range(4):
            dst[j, 0], dst[3 - j, 1] = before.astype(BF16), after.astype(BF16)
            if j < 3:
                before = before * p1 + buf[j, 0].astype(F32)
                after = after * p1 + buf[3 - j, 1].astype(F32)

    def put(ref, pair):
        ref[0], ref[1] = pair[0].astype(BF16), pair[1].astype(BF16)

    copies = []
    for k, d in enumerate((1, 2, 3)):
        part = send_x.at[:, :, lanes_of(((px + d) % 4) * quarter, quarter)]
        copies.append(push(part, buf_x.at[px], sem_x, k, mates_x[k]))
    buf_x[px] = send_x[:, :, lanes_of(px * quarter, quarter)]
    rate_x = rate_lanes[:, lanes_of(c * half + px * quarter, quarter)]
    rate_y = rate_lanes[:, lanes_of(c * half + px * quarter + py * eighth, eighth)]
    local_pieces(2, 4)
    for copy in copies:
        copy.wait()
    put(send_y, total(buf_x, 256, rate_x))
    copies = []
    for k, d in enumerate((1, 2, 3)):
        part = send_y.at[:, :, lanes_of(((py + d) % 4) * eighth, eighth)]
        copies.append(push(part, buf_y.at[py], sem_y, k, mates_y[k]))
    buf_y[py] = send_y[:, :, lanes_of(py * eighth, eighth)]
    push_halo(0, 3)
    local_pieces(4, 6)
    for copy in copies:
        copy.wait()
    put(send_z, total(buf_y, 1024, rate_y))
    copies = [push(send_z, buf_z.at[pz], sem_z, k, mates_z[k]) for k in range(3)]
    buf_z[pz] = send_z[...]
    local_pieces(6, 8)
    for copy in copies:
        copy.wait()
    zero = jnp.zeros_like(rate_y)
    exclusive(buf_z, 4096, rate_y, zero, zero, push_z)
    exclusive(buf_y, 1024, rate_y, push_z[pz, 0].astype(F32), push_z[pz, 1].astype(F32), push_y)
    copies = []
    for k, d in enumerate((1, 2, 3)):
        copies.append(push(push_y.at[(py + d) % 4], buf_w.at[py], sem_w, k, mates_y[k]))
    buf_w[py] = push_y[py]
    over_blocks(medium_tables, 0, blocks // 2)
    for copy in copies:
        copy.wait()
    before = jnp.concatenate([buf_w[j, 0] for j in range(4)], axis=1).astype(F32)
    after = jnp.concatenate([buf_w[j, 1] for j in range(4)], axis=1).astype(F32)
    exclusive(buf_x, 256, rate_x, before, after, push_x)
    copies = []
    for k, d in enumerate((1, 2, 3)):
        copies.append(push(push_x.at[(px + d) % 4], buf_r.at[px], sem_r, k, mates_x[k]))
    buf_r[px] = push_x[px]
    over_blocks(medium_tables, blocks // 2, blocks // 2)
    for copy in copies:
        copy.wait()
    for j in range(4):
        lanes = pl.ds(j * quarter, quarter)
        part = slice(j * quarter, (j + 1) * quarter)
        early_a, late_b = buf_r[j, 0].astype(F32), buf_r[j, 1].astype(F32)
        late_a = first_a[:, part] + step[:, part] * early_a
        early_b = second_b[:, part] + step[:, part] * late_b
        push_c[0, :, lanes] = jnp.where(c == 0, late_a, early_a).astype(BF16)
        push_c[1, :, lanes] = jnp.where(c == 0, late_b, early_b).astype(BF16)
        keep = lanes_of(c * half + j * quarter, quarter)
        states[0, :, keep] = jnp.where(c == 0, early_a, late_a).astype(BF16)
        states[1, :, keep] = jnp.where(c == 0, early_b, late_b).astype(BF16)
    push(push_c, states.at[:, :, mine], sem_d, 0, partner).wait()
    near_copy = push(states.at[1], near, sem_n, 0, previous)
    push_halo(3, SPLIT)

    for u in range(UNROLL):
        rows[u, L : L + 8, :] = jnp.zeros((8, L), F32)

    upper = jnp.concatenate([(lane >= sub).astype(F32).astype(BF16)] * G, axis=1)
    lower = jnp.concatenate([(lane < sub).astype(F32).astype(BF16)] * G, axis=1)

    def adjoint_filters(b, u):
        cols = lanes_of(b * L, L)
        into = (weight[pl.ds(b, 1), :] * jnp.exp(-rate[pl.ds(b, 1), :] * (L - sub).astype(F32))).astype(BF16)
        close = states[1, :, cols].astype(F32)
        far = jnp.where(last, 0.0, near[:, cols].astype(F32))
        entering = spread_groups(jnp.concatenate([close, far], axis=1)).astype(BF16)
        beyond = jnp.where(last, 0.0, halo[:, cols].astype(F32))
        inside = jnp.concatenate([adj[:, cols].astype(F32), beyond], axis=1)
        grad_b = (inside + matmul(into, entering)).astype(BF16)
        table = circ[b]
        tables = jnp.concatenate([table * upper, table * lower], axis=0)
        both = matmul(tables, masked_stack(grad_b))
        grad_a = (both[:L, :L] + both[L:, L:]).astype(BF16)
        rows[u, 0:L, :] = grad_a.astype(F32)
        head[:, cols] = rows[u, 0:8, :].astype(BF16)
        tail[:, cols] = rows[u, 112:128, :]
        taps_s = short[:, cols].astype(F32)
        sum_k = taps_s[0:1, :] * rows[u, 0:L, :]
        for k in range(1, 7):
            sum_k += taps_s[k : k + 1, :] * rows[u, k : k + L, :]
        grad_out[:, cols] = sum_k.astype(BF16)

    def gate_gradient(b, u):
        cols = lanes_of(b * L, L)
        into = (weight[pl.ds(b, 1), :] * jnp.exp(-rate[pl.ds(b, 1), :] * (sub + 1).astype(F32))).astype(BF16)
        entering = spread_groups(states[0, :, cols].astype(F32)).astype(BF16)
        full = matmul(jnp.concatenate([flip, into], axis=1), jnp.concatenate([conv[:, cols], entering], axis=0))
        full = (full + direct[pl.ds(b, 1), :] * x[:, cols].astype(F32)).astype(BF16)
        gate_out[:, cols] = (og[:, cols].astype(F32) * full.astype(F32)).astype(BF16)

    head_copies, stores = [], []

    def store(src, dst, sem):
        stores.append(pltpu.make_async_copy(src, dst, sem))
        stores[-1].start()

    def gate_pieces(first, stop):
        for k in range(first, stop):
            cols = slice(k * wide, (k + 1) * wide)
            over_blocks(gate_gradient, k * size, size)
            store(gate_out.at[:, cols], gate_done.at[:, cols], sem_o.at[0, k])

    gate_pieces(0, 6)
    near_copy.wait()
    for k in range(SPLIT):
        start = piece(k, 1 - c)
        cols = lanes_of(start * wide, wide)
        halo_copies[k].wait()
        over_blocks(adjoint_filters, start * size, size)
        head_copies.append(push(head.at[:, cols], head_next.at[:, cols], sem_e, k, previous))
        store(grad_out.at[0:112, cols], grad_done.at[0:112, cols], sem_o.at[1, k])
    gate_pieces(6, SPLIT)
    for copy in head_copies:
        copy.wait()

    def last_rows(b, u):
        cols = lanes_of(b * L, L)
        ends[u, 0:16, :] = tail[:, cols]
        ends[u, 16:24, :] = jnp.where(last, 0.0, head_next[:, cols].astype(F32))
        taps_s = short[:, cols].astype(F32)
        sum_k = taps_s[0:1, :] * ends[u, 0:16, :]
        for k in range(1, 7):
            sum_k += taps_s[k : k + 1, :] * ends[u, k : k + 16, :]
        grad_out[112:128, cols] = sum_k.astype(BF16)

    over_blocks(last_rows, 0, blocks)
    stores.append(pltpu.make_async_copy(grad_out.at[112:128, :], grad_done.at[112:128, :], sem_o.at[2, 0]))
    stores[-1].start()
    for copy in stores:
        copy.wait()


def on_device(x, gate, og, short_filter, medium_filter, decay_rates, residues, direct_term):
    channels = x.shape[1]
    groups = channels // 16
    rows = decay_rates.shape[0] // G
    half, quarter, eighth = channels // 2, channels // 8, channels // 32
    wide = pltpu.VMEM((L, channels), BF16)
    vmem, dma = pltpu.VMEM, pltpu.SemaphoreType.DMA
    return pl.pallas_call(
        kernel,
        out_shape=(jax.ShapeDtypeStruct(x.shape, BF16),) * 2,
        in_specs=[pl.BlockSpec(memory_space=pl.ANY)] * 3 + [pl.BlockSpec(memory_space=pltpu.VMEM)] * 5,
        out_specs=(pl.BlockSpec(memory_space=pl.ANY),) * 2,
        scratch_shapes=[
            wide, wide, wide, wide, wide,
            vmem((16, groups), F32),
            vmem((16, groups), F32),
            vmem((L, groups), BF16),
            vmem((channels // L, L, G * L), BF16),
            vmem((2 * rows, L), F32),
            vmem((2 * rows, L), F32),
            vmem((2 * rows, L), F32),
            vmem((7, channels), BF16),
            vmem((groups, L), F32),
            wide,
            vmem((16, channels), F32),
            vmem((2, 16, channels), BF16),
            vmem((16, channels), BF16),
            wide,
            wide,
            wide,
            vmem((2, 16, half), BF16),
            vmem((2, 16, half), BF16),
            vmem((4, 2, 16, quarter), BF16),
            vmem((2, 16, quarter), BF16),
            vmem((4, 2, 16, eighth), BF16),
            vmem((2, 16, eighth), BF16),
            vmem((4, 2, 16, eighth), BF16),
            vmem((4, 2, 16, eighth), BF16),
            vmem((4, 2, 16, eighth), BF16),
            vmem((4, 2, 16, eighth), BF16),
            vmem((4, 2, 16, quarter), BF16),
            vmem((4, 2, 16, quarter), BF16),
            vmem((2, 16, half), BF16),
            vmem((2, 16, channels), BF16),
            vmem((8, channels), BF16),
            vmem((8, channels), BF16),
            vmem((16, channels), F32),
            vmem((UNROLL, L + 8, L), F32),
            vmem((UNROLL, 24, L), F32),
            dma((3,)), dma((3, SPLIT)), dma((2, 5)), dma((5,)), dma((2, 1)), dma((2, 1)), dma((2, 3)), dma((2, 3)), dma((2, 3)),
            dma((2, 3)), dma((2, 3)), dma((2, 1)), dma((2, SPLIT)), dma((2, SPLIT)),
        ],
        compiler_params=pltpu.CompilerParams(
            collective_id=0, has_side_effects=True, vmem_limit_bytes=58 * 2**20
        ),
    )(
        x,
        gate,
        og,
        decay_rates.T,
        residues.T,
        direct_term.reshape(rows, L),
        short_filter,
        medium_filter,
    )


def solution(mesh):
    placed = (
        P(("ctx", "ch"), None),
        P(("ctx", "ch"), None),
        P(("ctx", "ch"), None),
        P(None, "ch"),
        P(None, "ch"),
        P("ch", None),
        P("ch", None),
        P("ch"),
    )
    return jax.shard_map(
        on_device,
        mesh=mesh,
        in_specs=placed,
        out_specs=(P(("ctx", "ch"), None), P(("ctx", "ch"), None)),
        check_vma=False,
    )
```

```python
import functools

import jax
import jax.numpy as jnp
from jax import lax
from jax.experimental import pallas as pl
from jax.experimental.pallas import tpu as pltpu
from jax.sharding import PartitionSpec as P

MESH = pl.DeviceIdType.MESH
F32 = jnp.float32
BF16 = jnp.bfloat16
L = 128
G = 8
SPLIT = 8
UNROLL = 4


def iota(shape, dim):
    return lax.broadcasted_iota(jnp.int32, shape, dim)


def matmul(a, b):
    return lax.dot_general(a, b, (((1,), (0,)), ((), ())), preferred_element_type=F32)


def column(row):
    return jnp.broadcast_to(row, (L, L)).T


def own_groups(block):
    shape = block.shape
    keep = (iota(shape, 0) // 16) == ((iota(shape, 1) % L) // 16)
    return jnp.sum(jnp.where(keep, block, 0.0).reshape(G, 16, shape[1]), axis=0)


def spread_groups(states):
    shape = (L, states.shape[1])
    keep = (iota(shape, 0) // 16) == ((iota(shape, 1) % L) // 16)
    return jnp.where(keep, jnp.concatenate([states] * G, axis=0), 0.0)


def masked_stack(data):
    lanes = (iota((1, data.shape[1]), 1) % L) // 16
    return jnp.concatenate([data * (lanes == g).astype(F32).astype(BF16) for g in range(G)], axis=0)


def circulant(row):
    return pltpu.roll(jnp.broadcast_to(row, (L, L)), 0, 1, stride=1, stride_axis=0)


def kernel(
    x_in, gate_in, og_in, rate_in, weight_in, direct_in, short_in, medium_in, grad_done, gate_done,
    x, gate, og, grad_out, gate_out, rate_by_group, weight_by_group, medium_raw, circ,
    rate, weight, direct, short, medium, grad_y, rate_lanes, sums, near, conv, adj, halo,
    buf_c, send_x, buf_x, send_y, buf_y, push_y, buf_w, push_x, buf_r, push_c, states,
    head, head_next, tail, rows, ends,
    sem_i, sem_o, sem_p, sem_l, sem_n, sem_c, sem_x, sem_y, sem_w, sem_r, sem_d, sem_h, sem_e,
):
    channels = x_in.shape[1]
    blocks = channels // L
    wide = channels // SPLIT
    half, quarter = channels // 2, channels // 8
    ctx, c = lax.axis_index("ctx"), lax.axis_index("ch")
    px, py, pz = ctx % 4, (ctx // 4) % 4, ctx // 16
    me = ctx * 2 + c
    before_me, after_me = (me + 127) % 128, (me + 1) % 128
    last = me == 127

    def at(z_, y_, x_):
        return (z_ * 16 + y_ * 4 + x_, c)

    partner = (ctx, 1 - c)
    previous = (before_me // 2, before_me % 2)
    following = (after_me // 2, after_me % 2)
    mates_x = [at(pz, py, (px + d) % 4) for d in (1, 2, 3)]
    row = pz * 4 + py
    others = [(row + d) % 16 for d in range(1, 16)]
    mates_row = [at(other // 4, other % 4, px) for other in others]
    loads = []
    for k, (src, dst) in enumerate([(x_in, x), (gate_in, gate), (og_in, og)]):
        loads.append(pltpu.make_async_copy(src, dst, sem_i.at[k]))
        loads[-1].start()
    barrier = pltpu.get_barrier_semaphore()
    for mate in [partner, following] + mates_x + mates_row:
        pl.semaphore_signal(barrier, inc=1, device_id=mate, device_id_type=MESH)

    def push(src, dst, sem, k, mate):
        copy = pltpu.make_async_remote_copy(
            src, dst, sem.at[0, k], sem.at[1, k], device_id=mate, device_id_type=MESH
        )
        copy.start()
        return copy

    def lanes_of(start, size):
        return pl.ds(pl.multiple_of(start, L), size)

    mine, theirs = lanes_of(c * half, half), lanes_of((1 - c) * half, half)
    count = rate_in.shape[1]
    groups_mine = lanes_of(c * count, count)
    places = [
        (rate_in, rate_by_group.at[:, groups_mine]),
        (weight_in, weight_by_group.at[:, groups_mine]),
        (medium_in, medium_raw.at[:, groups_mine]),
        (direct_in, direct.at[pl.ds(pl.multiple_of(c * direct_in.shape[0], 8), direct_in.shape[0]), :]),
        (short_in, short.at[:, mine]),
    ]
    here = []
    for k, (own, place) in enumerate(places):
        here.append(pltpu.make_async_copy(own, place, sem_l.at[k]))
        here[-1].start()
    for copy in here + loads:
        copy.wait()

    lane, sub = iota((L, L), 1), iota((L, L), 0)
    flip = (lane + sub == 127).astype(F32).astype(BF16)

    def over_blocks(body, start, size):
        def step(i, _):
            for u in range(UNROLL):
                body(start + i * UNROLL + u, u)
            return 0

        lax.fori_loop(0, size // UNROLL, step, 0)

    def block_sums(b, u):
        cols = lanes_of(b * L, L)
        tile = lanes_of((b // 16) * L, L)
        pick = (b % 16) * G + iota((16, L), 1) // 16
        diagonal = iota((16, L), 0) == iota((16, L), 1) % 16
        rate_here = jnp.take_along_axis(rate_by_group[:, tile], pick, axis=1)
        weight_here = jnp.take_along_axis(weight_by_group[:, tile], pick, axis=1)
        rate_row = jnp.sum(jnp.where(diagonal, rate_here, 0.0), axis=0, keepdims=True)
        weight_row = jnp.sum(jnp.where(diagonal, weight_here, 0.0), axis=0, keepdims=True)
        rate_lanes[:, cols] = rate_here
        rate[pl.ds(b, 1), :] = rate_row
        weight[pl.ds(b, 1), :] = weight_row
        rate_col = column(rate_row)
        ahead = jnp.exp(-rate_col * (127 - lane).astype(F32)).astype(BF16)
        behind = jnp.exp(-rate_col * lane.astype(F32)).astype(BF16)
        y = (og[:, cols].astype(F32) * gate[:, cols].astype(F32)).astype(BF16)
        grad_y[:, cols] = y
        both = matmul(jnp.concatenate([ahead, behind], axis=0), jnp.concatenate([x[:, cols], y], axis=1))
        sums[0, :, cols] = own_groups(both[:L, :L]).astype(BF16)
        sums[1, :, cols] = own_groups(both[L:, L:]).astype(BF16)

    def local_products(b, u):
        cols = lanes_of(b * L, L)
        decay = jnp.exp(-column(rate[pl.ds(b, 1), :]) * lane.astype(F32))
        k = jnp.sum((column(weight[pl.ds(b, 1), :]) * decay).reshape(G, 16, L), axis=1)
        back = matmul(flip, x[:, cols]).astype(BF16)
        table = [jnp.where(lane >= sub, circulant(k[g : g + 1, :]), 0.0).astype(BF16) for g in range(G)]
        y = grad_y[:, cols]
        data = jnp.concatenate([back, y], axis=1)
        both = matmul(jnp.concatenate(table, axis=1), masked_stack(data))
        conv[:, cols] = both[:, :L].astype(BF16)
        adj[:, cols] = (both[:, L:] + direct[pl.ds(b, 1), :] * y.astype(F32)).astype(BF16)

    def medium_tables(b, u):
        m = medium[pl.ds(pl.multiple_of(b * G, G), G), :]
        for g in range(G):
            circ[b, :, g * L : g * L + L] = circulant(m[g : g + 1, :]).astype(BF16)

    size = blocks // SPLIT
    halo_copies = []

    def piece(k, core):
        return (core * (SPLIT // 2) + k) % SPLIT

    def local_pieces(first, stop):
        for k in range(first, stop):
            over_blocks(local_products, piece(k, c) * size, size)

    def push_halo(first, stop):
        for k in range(first, stop):
            cols = lanes_of(piece(k, c) * wide, wide)
            halo_copies.append(push(adj.at[:, cols], halo.at[:, cols], sem_h, k, previous))

    over_blocks(block_sums, c * (blocks // 2), blocks // 2)
    pl.semaphore_wait(barrier, 20)
    gathers = [push(own, place, sem_p, k, partner) for k, (own, place) in enumerate(places)]
    local_pieces(0, 1)
    push_halo(0, 1)
    for copy in gathers:
        copy.wait()
    over_blocks(block_sums, (1 - c) * (blocks // 2), blocks // 2)
    first_copy = push(sums.at[:, :, theirs], buf_c, sem_c, 0, partner)
    for k in range(medium.shape[0] // L):
        medium[k * L : k * L + L, :] = medium_raw[:, k * L : k * L + L].astype(F32).T
    local_pieces(1, 2)

    step = jnp.exp(-rate_lanes[:, mine] * 128.0)
    own = sums[:, :, mine].astype(F32)
    first_copy.wait()
    other = buf_c[...].astype(F32)
    first_a, second_a = jnp.where(c == 0, own[0], other[0]), jnp.where(c == 0, other[0], own[0])
    first_b, second_b = jnp.where(c == 0, own[1], other[1]), jnp.where(c == 0, other[1], own[1])
    send_x[0] = (second_a + step * first_a).astype(BF16)
    send_x[1] = (first_b + step * second_b).astype(BF16)

    def total(buf, span, rate_):
        p1 = jnp.exp(-rate_ * float(span))
        sum_a, sum_b = buf[0, 0].astype(F32), buf[3, 1].astype(F32)
        for j in (1, 2, 3):
            sum_a = sum_a * p1 + buf[j, 0].astype(F32)
            sum_b = sum_b * p1 + buf[3 - j, 1].astype(F32)
        return sum_a, sum_b

    def exclusive(buf, span, rate_, before, after, dst):
        p1 = jnp.exp(-rate_ * float(span))
        for j in range(4):
            dst[j, 0], dst[3 - j, 1] = before.astype(BF16), after.astype(BF16)
            if j < 3:
                before = before * p1 + buf[j, 0].astype(F32)
                after = after * p1 + buf[3 - j, 1].astype(F32)

    def put(ref, pair):
        ref[0], ref[1] = pair[0].astype(BF16), pair[1].astype(BF16)

    copies = []
    for k, d in enumerate((1, 2, 3)):
        part = send_x.at[:, :, lanes_of(((px + d) % 4) * quarter, quarter)]
        copies.append(push(part, buf_x.at[px], sem_x, k, mates_x[k]))
    buf_x[px] = send_x[:, :, lanes_of(px * quarter, quarter)]
    rate_x = rate_lanes[:, lanes_of(c * half + px * quarter, quarter)]
    rate_row = rate_lanes[:, lanes_of(c * half + px * quarter + (row % 8) * L, L)]
    local_pieces(2, 4)
    for copy in copies:
        copy.wait()
    put(send_y, total(buf_x, 256, rate_x))
    copies = []
    for k, other in enumerate(others):
        part = send_y.at[other // 8, :, lanes_of((other % 8) * L, L)]
        copies.append(push(part, buf_y.at[row], sem_y, k, mates_row[k]))
    buf_y[row] = send_y[row // 8, :, lanes_of((row % 8) * L, L)]
    push_halo(1, 3)
    local_pieces(4, 7)
    for copy in copies:
        copy.wait()
    p1 = jnp.exp(-rate_row * 1024.0)
    state = jnp.zeros_like(rate_row)
    for j in range(16):
        place = jnp.where(row < 8, j, 15 - j)
        push_y[place] = state.astype(BF16)
        state = state * p1 + buf_y[place].astype(F32)
    copies = []
    for k, other in enumerate(others):
        copies.append(push(push_y.at[other], buf_w.at[row], sem_w, k, mates_row[k]))
    buf_w[row] = push_y[row]
    push_halo(3, 5)
    local_pieces(7, SPLIT)
    over_blocks(medium_tables, 0, blocks // 2)
    for copy in copies:
        copy.wait()
    before = jnp.concatenate([buf_w[j] for j in range(8)], axis=1).astype(F32)
    after = jnp.concatenate([buf_w[j + 8] for j in range(8)], axis=1).astype(F32)
    exclusive(buf_x, 256, rate_x, before, after, push_x)
    copies = []
    for k, d in enumerate((1, 2, 3)):
        copies.append(push(push_x.at[(px + d) % 4], buf_r.at[px], sem_r, k, mates_x[k]))
    buf_r[px] = push_x[px]
    over_blocks(medium_tables, blocks // 2, blocks // 2)
    for copy in copies:
        copy.wait()
    for j in range(4):
        lanes = pl.ds(j * quarter, quarter)
        part = slice(j * quarter, (j + 1) * quarter)
        early_a, late_b = buf_r[j, 0].astype(F32), buf_r[j, 1].astype(F32)
        late_a = first_a[:, part] + step[:, part] * early_a
        early_b = second_b[:, part] + step[:, part] * late_b
        push_c[0, :, lanes] = jnp.where(c == 0, late_a, early_a).astype(BF16)
        push_c[1, :, lanes] = jnp.where(c == 0, late_b, early_b).astype(BF16)
        keep = lanes_of(c * half + j * quarter, quarter)
        states[0, :, keep] = jnp.where(c == 0, early_a, late_a).astype(BF16)
        states[1, :, keep] = jnp.where(c == 0, early_b, late_b).astype(BF16)
    push(push_c, states.at[:, :, mine], sem_d, 0, partner).wait()
    near_copy = push(states.at[1], near, sem_n, 0, previous)
    push_halo(5, SPLIT)

    for u in range(UNROLL):
        rows[u, L : L + 8, :] = jnp.zeros((8, L), F32)

    upper = jnp.concatenate([(lane >= sub).astype(F32).astype(BF16)] * G, axis=1)
    lower = jnp.concatenate([(lane < sub).astype(F32).astype(BF16)] * G, axis=1)

    def adjoint_filters(b, u):
        cols = lanes_of(b * L, L)
        into = (weight[pl.ds(b, 1), :] * jnp.exp(-rate[pl.ds(b, 1), :] * (L - sub).astype(F32))).astype(BF16)
        close = states[1, :, cols].astype(F32)
        far = jnp.where(last, 0.0, near[:, cols].astype(F32))
        entering = spread_groups(jnp.concatenate([close, far], axis=1)).astype(BF16)
        beyond = jnp.where(last, 0.0, halo[:, cols].astype(F32))
        inside = jnp.concatenate([adj[:, cols].astype(F32), beyond], axis=1)
        grad_b = (inside + matmul(into, entering)).astype(BF16)
        table = circ[b]
        tables = jnp.concatenate([table * upper, table * lower], axis=0)
        both = matmul(tables, masked_stack(grad_b))
        grad_a = (both[:L, :L] + both[L:, L:]).astype(BF16)
        rows[u, 0:L, :] = grad_a.astype(F32)
        head[:, cols] = rows[u, 0:8, :].astype(BF16)
        tail[:, cols] = rows[u, 112:128, :]
        taps_s = short[:, cols].astype(F32)
        sum_k = taps_s[0:1, :] * rows[u, 0:L, :]
        for k in range(1, 7):
            sum_k += taps_s[k : k + 1, :] * rows[u, k : k + L, :]
        grad_out[:, cols] = sum_k.astype(BF16)

    def gate_gradient(b, u):
        cols = lanes_of(b * L, L)
        into = (weight[pl.ds(b, 1), :] * jnp.exp(-rate[pl.ds(b, 1), :] * (sub + 1).astype(F32))).astype(BF16)
        entering = spread_groups(states[0, :, cols].astype(F32)).astype(BF16)
        full = matmul(jnp.concatenate([flip, into], axis=1), jnp.concatenate([conv[:, cols], entering], axis=0))
        full = (full + direct[pl.ds(b, 1), :] * x[:, cols].astype(F32)).astype(BF16)
        gate_out[:, cols] = (og[:, cols].astype(F32) * full.astype(F32)).astype(BF16)

    head_copies, stores = [], []

    def store(src, dst, sem):
        stores.append(pltpu.make_async_copy(src, dst, sem))
        stores[-1].start()

    def gate_pieces(first, stop):
        for k in range(first, stop):
            cols = slice(k * wide, (k + 1) * wide)
            over_blocks(gate_gradient, k * size, size)
            store(gate_out.at[:, cols], gate_done.at[:, cols], sem_o.at[0, k])

    gate_pieces(0, 6)
    near_copy.wait()
    for k in range(SPLIT):
        start = piece(k, 1 - c)
        cols = lanes_of(start * wide, wide)
        halo_copies[k].wait()
        over_blocks(adjoint_filters, start * size, size)
        head_copies.append(push(head.at[:, cols], head_next.at[:, cols], sem_e, k, previous))
        store(grad_out.at[0:112, cols], grad_done.at[0:112, cols], sem_o.at[1, k])
    gate_pieces(6, SPLIT)
    for copy in head_copies:
        copy.wait()

    def last_rows(b, u):
        cols = lanes_of(b * L, L)
        ends[u, 0:16, :] = tail[:, cols]
        ends[u, 16:24, :] = jnp.where(last, 0.0, head_next[:, cols].astype(F32))
        taps_s = short[:, cols].astype(F32)
        sum_k = taps_s[0:1, :] * ends[u, 0:16, :]
        for k in range(1, 7):
            sum_k += taps_s[k : k + 1, :] * ends[u, k : k + 16, :]
        grad_out[112:128, cols] = sum_k.astype(BF16)

    over_blocks(last_rows, 0, blocks)
    stores.append(pltpu.make_async_copy(grad_out.at[112:128, :], grad_done.at[112:128, :], sem_o.at[2, 0]))
    stores[-1].start()
    for copy in stores:
        copy.wait()


def on_device(x, gate, og, short_filter, medium_filter, decay_rates, residues, direct_term):
    channels = x.shape[1]
    groups = channels // 16
    rows = decay_rates.shape[0] // G
    half, quarter = channels // 2, channels // 8
    wide = pltpu.VMEM((L, channels), BF16)
    vmem, dma = pltpu.VMEM, pltpu.SemaphoreType.DMA
    return pl.pallas_call(
        kernel,
        out_shape=(jax.ShapeDtypeStruct(x.shape, BF16),) * 2,
        in_specs=[pl.BlockSpec(memory_space=pl.ANY)] * 3 + [pl.BlockSpec(memory_space=pltpu.VMEM)] * 5,
        out_specs=(pl.BlockSpec(memory_space=pl.ANY),) * 2,
        scratch_shapes=[
            wide, wide, wide, wide, wide,
            vmem((16, groups), F32),
            vmem((16, groups), F32),
            vmem((L, groups), BF16),
            vmem((channels // L, L, G * L), BF16),
            vmem((2 * rows, L), F32),
            vmem((2 * rows, L), F32),
            vmem((2 * rows, L), F32),
            vmem((7, channels), BF16),
            vmem((groups, L), F32),
            wide,
            vmem((16, channels), F32),
            vmem((2, 16, channels), BF16),
            vmem((16, channels), BF16),
            wide,
            wide,
            wide,
            vmem((2, 16, half), BF16),
            vmem((2, 16, half), BF16),
            vmem((4, 2, 16, quarter), BF16),
            vmem((2, 16, quarter), BF16),
            vmem((16, 16, L), BF16),
            vmem((16, 16, L), BF16),
            vmem((16, 16, L), BF16),
            vmem((4, 2, 16, quarter), BF16),
            vmem((4, 2, 16, quarter), BF16),
            vmem((2, 16, half), BF16),
            vmem((2, 16, channels), BF16),
            vmem((8, channels), BF16),
            vmem((8, channels), BF16),
            vmem((16, channels), F32),
            vmem((UNROLL, L + 8, L), F32),
            vmem((UNROLL, 24, L), F32),
            dma((3,)), dma((3, SPLIT)), dma((2, 5)), dma((5,)), dma((2, 1)), dma((2, 1)), dma((2, 3)), dma((2, 15)),
            dma((2, 15)), dma((2, 3)), dma((2, 1)), dma((2, SPLIT)), dma((2, SPLIT)),
        ],
        compiler_params=pltpu.CompilerParams(
            collective_id=0, has_side_effects=True, vmem_limit_bytes=58 * 2**20
        ),
    )(
        x,
        gate,
        og,
        decay_rates.T,
        residues.T,
        direct_term.reshape(rows, L),
        short_filter,
        medium_filter,
    )


def solution(mesh):
    placed = (
        P(("ctx", "ch"), None),
        P(("ctx", "ch"), None),
        P(("ctx", "ch"), None),
        P(None, "ch"),
        P(None, "ch"),
        P("ch", None),
        P("ch", None),
        P("ch"),
    )
    return jax.shard_map(
        on_device,
        mesh=mesh,
        in_specs=placed,
        out_specs=(P(("ctx", "ch"), None), P(("ctx", "ch"), None)),
        check_vma=False,
    )
```

```python
import functools

import jax
import jax.numpy as jnp
from jax import lax
from jax.experimental import pallas as pl
from jax.experimental.pallas import tpu as pltpu
from jax.sharding import PartitionSpec as P

MESH = pl.DeviceIdType.MESH
F32 = jnp.float32
BF16 = jnp.bfloat16
L = 128
G = 8
SPLIT = 8
UNROLL = 4


def iota(shape, dim):
    return lax.broadcasted_iota(jnp.int32, shape, dim)


def matmul(a, b):
    return lax.dot_general(a, b, (((1,), (0,)), ((), ())), preferred_element_type=F32)


def column(row):
    return jnp.broadcast_to(row, (L, L)).T


def own_groups(block):
    shape = block.shape
    keep = (iota(shape, 0) // 16) == ((iota(shape, 1) % L) // 16)
    return jnp.sum(jnp.where(keep, block, 0.0).reshape(G, 16, shape[1]), axis=0)


def spread_groups(states):
    shape = (L, states.shape[1])
    keep = (iota(shape, 0) // 16) == ((iota(shape, 1) % L) // 16)
    return jnp.where(keep, jnp.concatenate([states] * G, axis=0), 0.0)


def masked_stack(data):
    lanes = (iota((1, data.shape[1]), 1) % L) // 16
    return jnp.concatenate([data * (lanes == g).astype(F32).astype(BF16) for g in range(G)], axis=0)


def circulant(row):
    return pltpu.roll(jnp.broadcast_to(row, (L, L)), 0, 1, stride=1, stride_axis=0)


def kernel(
    x_in, gate_in, og_in, rate_in, weight_in, direct_in, short_in, medium_in, grad_done, gate_done,
    x, gate, og, grad_out, gate_out, rate_by_group, weight_by_group, medium_raw, circ,
    rate, weight, direct, short, medium, grad_y, rate_lanes, sums, near, conv, adj, halo,
    buf_c, send_x, buf_x, send_y, buf_y, push_y, buf_w, push_x, buf_r, push_c, states,
    head, head_next, tail, rows, ends,
    sem_i, sem_o, sem_p, sem_l, sem_n, sem_c, sem_x, sem_y, sem_w, sem_r, sem_d, sem_h, sem_e,
):
    channels = x_in.shape[1]
    blocks = channels // L
    wide = channels // SPLIT
    half, quarter = channels // 2, channels // 8
    ctx, c = lax.axis_index("ctx"), lax.axis_index("ch")
    px, py, pz = ctx % 4, (ctx // 4) % 4, ctx // 16
    me = ctx * 2 + c
    before_me, after_me = (me + 127) % 128, (me + 1) % 128
    last = me == 127

    def at(z_, y_, x_):
        return (z_ * 16 + y_ * 4 + x_, c)

    partner = (ctx, 1 - c)
    previous = (before_me // 2, before_me % 2)
    following = (after_me // 2, after_me % 2)
    mates_x = [at(pz, py, (px + d) % 4) for d in (1, 2, 3)]
    row = pz * 4 + py
    others = [(row + d) % 16 for d in range(1, 16)]
    mates_row = [at(other // 4, other % 4, px) for other in others]
    loads = []
    for k, (src, dst) in enumerate([(x_in, x), (gate_in, gate), (og_in, og)]):
        loads.append(pltpu.make_async_copy(src, dst, sem_i.at[k]))
        loads[-1].start()
    barrier = pltpu.get_barrier_semaphore()
    for mate in [partner, following] + mates_x + mates_row:
        pl.semaphore_signal(barrier, inc=1, device_id=mate, device_id_type=MESH)

    def push(src, dst, sem, k, mate):
        copy = pltpu.make_async_remote_copy(
            src, dst, sem.at[0, k], sem.at[1, k], device_id=mate, device_id_type=MESH
        )
        copy.start()
        return copy

    def lanes_of(start, size):
        return pl.ds(pl.multiple_of(start, L), size)

    mine, theirs = lanes_of(c * half, half), lanes_of((1 - c) * half, half)
    count = rate_in.shape[1]
    groups_mine = lanes_of(c * count, count)
    places = [
        (rate_in, rate_by_group.at[:, groups_mine]),
        (weight_in, weight_by_group.at[:, groups_mine]),
        (medium_in, medium_raw.at[:, groups_mine]),
        (direct_in, direct.at[pl.ds(pl.multiple_of(c * direct_in.shape[0], 8), direct_in.shape[0]), :]),
        (short_in, short.at[:, mine]),
    ]
    here = []
    for k, (own, place) in enumerate(places):
        here.append(pltpu.make_async_copy(own, place, sem_l.at[k]))
        here[-1].start()
    for copy in here + loads:
        copy.wait()

    lane, sub = iota((L, L), 1), iota((L, L), 0)
    flip = (lane + sub == 127).astype(F32).astype(BF16)

    def over_blocks(body, start, size):
        def step(i, _):
            for u in range(UNROLL):
                body(start + i * UNROLL + u, u)
            return 0

        lax.fori_loop(0, size // UNROLL, step, 0)

    def block_sums(b, u):
        cols = lanes_of(b * L, L)
        tile = lanes_of((b // 16) * L, L)
        pick = (b % 16) * G + iota((16, L), 1) // 16
        diagonal = iota((16, L), 0) == iota((16, L), 1) % 16
        rate_here = jnp.take_along_axis(rate_by_group[:, tile], pick, axis=1)
        weight_here = jnp.take_along_axis(weight_by_group[:, tile], pick, axis=1)
        rate_row = jnp.sum(jnp.where(diagonal, rate_here, 0.0), axis=0, keepdims=True)
        weight_row = jnp.sum(jnp.where(diagonal, weight_here, 0.0), axis=0, keepdims=True)
        rate_lanes[:, cols] = rate_here
        rate[pl.ds(b, 1), :] = rate_row
        weight[pl.ds(b, 1), :] = weight_row
        rate_col = column(rate_row)
        ahead = jnp.exp(-rate_col * (127 - lane).astype(F32)).astype(BF16)
        behind = jnp.exp(-rate_col * lane.astype(F32)).astype(BF16)
        y = (og[:, cols].astype(F32) * gate[:, cols].astype(F32)).astype(BF16)
        grad_y[:, cols] = y
        both = matmul(jnp.concatenate([ahead, behind], axis=0), jnp.concatenate([x[:, cols], y], axis=1))
        sums[0, :, cols] = own_groups(both[:L, :L]).astype(BF16)
        sums[1, :, cols] = own_groups(both[L:, L:]).astype(BF16)

    def local_products(b, u):
        cols = lanes_of(b * L, L)
        decay = jnp.exp(-column(rate[pl.ds(b, 1), :]) * lane.astype(F32))
        k = jnp.sum((column(weight[pl.ds(b, 1), :]) * decay).reshape(G, 16, L), axis=1)
        back = matmul(flip, x[:, cols]).astype(BF16)
        table = [jnp.where(lane >= sub, circulant(k[g : g + 1, :]), 0.0).astype(BF16) for g in range(G)]
        y = grad_y[:, cols]
        data = jnp.concatenate([back, y], axis=1)
        both = matmul(jnp.concatenate(table, axis=1), masked_stack(data))
        conv[:, cols] = both[:, :L].astype(BF16)
        adj[:, cols] = (both[:, L:] + direct[pl.ds(b, 1), :] * y.astype(F32)).astype(BF16)

    def medium_tables(b, u):
        m = medium[pl.ds(pl.multiple_of(b * G, G), G), :]
        for g in range(G):
            circ[b, :, g * L : g * L + L] = circulant(m[g : g + 1, :]).astype(BF16)

    size = blocks // SPLIT
    halo_copies = []

    def piece(k, core):
        return (core * (SPLIT // 2) + k) % SPLIT

    def local_pieces(first, stop):
        over_blocks(local_products, piece(first, c) * size, (stop - first) * size)

    def push_halo(first, stop):
        for k in range(first, stop):
            cols = lanes_of(piece(k, c) * wide, wide)
            halo_copies.append(push(adj.at[:, cols], halo.at[:, cols], sem_h, k, previous))

    over_blocks(block_sums, c * (blocks // 2), blocks // 2)
    pl.semaphore_wait(barrier, 20)
    gathers = [push(own, place, sem_p, k, partner) for k, (own, place) in enumerate(places)]
    local_pieces(0, 1)
    push_halo(0, 1)
    for copy in gathers:
        copy.wait()
    over_blocks(block_sums, (1 - c) * (blocks // 2), blocks // 2)
    first_copy = push(sums.at[:, :, theirs], buf_c, sem_c, 0, partner)
    for k in range(medium.shape[0] // L):
        medium[k * L : k * L + L, :] = medium_raw[:, k * L : k * L + L].astype(F32).T
    local_pieces(1, 2)

    step = jnp.exp(-rate_lanes[:, mine] * 128.0)
    own = sums[:, :, mine].astype(F32)
    first_copy.wait()
    other = buf_c[...].astype(F32)
    first_a, second_a = jnp.where(c == 0, own[0], other[0]), jnp.where(c == 0, other[0], own[0])
    first_b, second_b = jnp.where(c == 0, own[1], other[1]), jnp.where(c == 0, other[1], own[1])
    send_x[0] = (second_a + step * first_a).astype(BF16)
    send_x[1] = (first_b + step * second_b).astype(BF16)

    def total(buf, span, rate_):
        p1 = jnp.exp(-rate_ * float(span))
        sum_a, sum_b = buf[0, 0].astype(F32), buf[3, 1].astype(F32)
        for j in (1, 2, 3):
            sum_a = sum_a * p1 + buf[j, 0].astype(F32)
            sum_b = sum_b * p1 + buf[3 - j, 1].astype(F32)
        return sum_a, sum_b

    def exclusive(buf, span, rate_, before, after, dst):
        p1 = jnp.exp(-rate_ * float(span))
        for j in range(4):
            dst[j, 0], dst[3 - j, 1] = before.astype(BF16), after.astype(BF16)
            if j < 3:
                before = before * p1 + buf[j, 0].astype(F32)
                after = after * p1 + buf[3 - j, 1].astype(F32)

    def put(ref, pair):
        ref[0], ref[1] = pair[0].astype(BF16), pair[1].astype(BF16)

    copies = []
    for k, d in enumerate((1, 2, 3)):
        part = send_x.at[:, :, lanes_of(((px + d) % 4) * quarter, quarter)]
        copies.append(push(part, buf_x.at[px], sem_x, k, mates_x[k]))
    buf_x[px] = send_x[:, :, lanes_of(px * quarter, quarter)]
    rate_x = rate_lanes[:, lanes_of(c * half + px * quarter, quarter)]
    rate_row = rate_lanes[:, lanes_of(c * half + px * quarter + (row % 8) * L, L)]
    local_pieces(2, 4)
    for copy in copies:
        copy.wait()
    put(send_y, total(buf_x, 256, rate_x))
    copies = []
    for k, other in enumerate(others):
        part = send_y.at[other // 8, :, lanes_of((other % 8) * L, L)]
        copies.append(push(part, buf_y.at[row], sem_y, k, mates_row[k]))
    buf_y[row] = send_y[row // 8, :, lanes_of((row % 8) * L, L)]
    push_halo(1, 3)
    local_pieces(4, 7)
    for copy in copies:
        copy.wait()
    p1 = jnp.exp(-rate_row * 1024.0)
    state = jnp.zeros_like(rate_row)
    for j in range(16):
        place = jnp.where(row < 8, j, 15 - j)
        push_y[place] = state.astype(BF16)
        state = state * p1 + buf_y[place].astype(F32)
    copies = []
    for k, other in enumerate(others):
        copies.append(push(push_y.at[other], buf_w.at[row], sem_w, k, mates_row[k]))
    buf_w[row] = push_y[row]
    push_halo(3, 5)
    local_pieces(7, SPLIT)
    over_blocks(medium_tables, 0, blocks // 2)
    for copy in copies:
        copy.wait()
    before = jnp.concatenate([buf_w[j] for j in range(8)], axis=1).astype(F32)
    after = jnp.concatenate([buf_w[j + 8] for j in range(8)], axis=1).astype(F32)
    exclusive(buf_x, 256, rate_x, before, after, push_x)
    copies = []
    for k, d in enumerate((1, 2, 3)):
        copies.append(push(push_x.at[(px + d) % 4], buf_r.at[px], sem_r, k, mates_x[k]))
    buf_r[px] = push_x[px]
    over_blocks(medium_tables, blocks // 2, blocks // 2)
    for copy in copies:
        copy.wait()
    for j in range(4):
        lanes = pl.ds(j * quarter, quarter)
        part = slice(j * quarter, (j + 1) * quarter)
        early_a, late_b = buf_r[j, 0].astype(F32), buf_r[j, 1].astype(F32)
        late_a = first_a[:, part] + step[:, part] * early_a
        early_b = second_b[:, part] + step[:, part] * late_b
        push_c[0, :, lanes] = jnp.where(c == 0, late_a, early_a).astype(BF16)
        push_c[1, :, lanes] = jnp.where(c == 0, late_b, early_b).astype(BF16)
        keep = lanes_of(c * half + j * quarter, quarter)
        states[0, :, keep] = jnp.where(c == 0, early_a, late_a).astype(BF16)
        states[1, :, keep] = jnp.where(c == 0, early_b, late_b).astype(BF16)
    push(push_c, states.at[:, :, mine], sem_d, 0, partner).wait()
    near_copy = push(states.at[1], near, sem_n, 0, previous)
    push_halo(5, SPLIT)

    for u in range(UNROLL):
        rows[u, L : L + 8, :] = jnp.zeros((8, L), F32)

    upper = jnp.concatenate([(lane >= sub).astype(F32).astype(BF16)] * G, axis=1)
    lower = jnp.concatenate([(lane < sub).astype(F32).astype(BF16)] * G, axis=1)

    def adjoint_filters(b, u):
        cols = lanes_of(b * L, L)
        into = (weight[pl.ds(b, 1), :] * jnp.exp(-rate[pl.ds(b, 1), :] * (L - sub).astype(F32))).astype(BF16)
        close = states[1, :, cols].astype(F32)
        far = jnp.where(last, 0.0, near[:, cols].astype(F32))
        entering = spread_groups(jnp.concatenate([close, far], axis=1)).astype(BF16)
        beyond = jnp.where(last, 0.0, halo[:, cols].astype(F32))
        inside = jnp.concatenate([adj[:, cols].astype(F32), beyond], axis=1)
        grad_b = (inside + matmul(into, entering)).astype(BF16)
        table = circ[b]
        tables = jnp.concatenate([table * upper, table * lower], axis=0)
        both = matmul(tables, masked_stack(grad_b))
        grad_a = (both[:L, :L] + both[L:, L:]).astype(BF16)
        rows[u, 0:L, :] = grad_a.astype(F32)
        head[:, cols] = rows[u, 0:8, :].astype(BF16)
        tail[:, cols] = rows[u, 112:128, :]
        taps_s = short[:, cols].astype(F32)
        sum_k = taps_s[0:1, :] * rows[u, 0:L, :]
        for k in range(1, 7):
            sum_k += taps_s[k : k + 1, :] * rows[u, k : k + L, :]
        grad_out[:, cols] = sum_k.astype(BF16)

    def gate_gradient(b, u):
        cols = lanes_of(b * L, L)
        into = (weight[pl.ds(b, 1), :] * jnp.exp(-rate[pl.ds(b, 1), :] * (sub + 1).astype(F32))).astype(BF16)
        entering = spread_groups(states[0, :, cols].astype(F32)).astype(BF16)
        full = matmul(jnp.concatenate([flip, into], axis=1), jnp.concatenate([conv[:, cols], entering], axis=0))
        full = (full + direct[pl.ds(b, 1), :] * x[:, cols].astype(F32)).astype(BF16)
        gate_out[:, cols] = (og[:, cols].astype(F32) * full.astype(F32)).astype(BF16)

    head_copies, stores = [], []

    def store(src, dst, sem):
        stores.append(pltpu.make_async_copy(src, dst, sem))
        stores[-1].start()

    def gate_pieces(first, stop):
        over_blocks(gate_gradient, first * size, (stop - first) * size)
        for k in range(first, stop):
            cols = slice(k * wide, (k + 1) * wide)
            store(gate_out.at[:, cols], gate_done.at[:, cols], sem_o.at[0, k])

    gate_pieces(0, 6)
    near_copy.wait()
    for k in range(SPLIT):
        start = piece(k, 1 - c)
        cols = lanes_of(start * wide, wide)
        halo_copies[k].wait()
        over_blocks(adjoint_filters, start * size, size)
        head_copies.append(push(head.at[:, cols], head_next.at[:, cols], sem_e, k, previous))
        store(grad_out.at[0:112, cols], grad_done.at[0:112, cols], sem_o.at[1, k])
    gate_pieces(6, SPLIT)
    for copy in head_copies:
        copy.wait()

    def last_rows(b, u):
        cols = lanes_of(b * L, L)
        ends[u, 0:16, :] = tail[:, cols]
        ends[u, 16:24, :] = jnp.where(last, 0.0, head_next[:, cols].astype(F32))
        taps_s = short[:, cols].astype(F32)
        sum_k = taps_s[0:1, :] * ends[u, 0:16, :]
        for k in range(1, 7):
            sum_k += taps_s[k : k + 1, :] * ends[u, k : k + 16, :]
        grad_out[112:128, cols] = sum_k.astype(BF16)

    over_blocks(last_rows, 0, blocks)
    stores.append(pltpu.make_async_copy(grad_out.at[112:128, :], grad_done.at[112:128, :], sem_o.at[2, 0]))
    stores[-1].start()
    for copy in stores:
        copy.wait()


def on_device(x, gate, og, short_filter, medium_filter, decay_rates, residues, direct_term):
    channels = x.shape[1]
    groups = channels // 16
    rows = decay_rates.shape[0] // G
    half, quarter = channels // 2, channels // 8
    wide = pltpu.VMEM((L, channels), BF16)
    vmem, dma = pltpu.VMEM, pltpu.SemaphoreType.DMA
    return pl.pallas_call(
        kernel,
        out_shape=(jax.ShapeDtypeStruct(x.shape, BF16),) * 2,
        in_specs=[pl.BlockSpec(memory_space=pl.ANY)] * 3 + [pl.BlockSpec(memory_space=pltpu.VMEM)] * 5,
        out_specs=(pl.BlockSpec(memory_space=pl.ANY),) * 2,
        scratch_shapes=[
            wide, wide, wide, wide, wide,
            vmem((16, groups), F32),
            vmem((16, groups), F32),
            vmem((L, groups), BF16),
            vmem((channels // L, L, G * L), BF16),
            vmem((2 * rows, L), F32),
            vmem((2 * rows, L), F32),
            vmem((2 * rows, L), F32),
            vmem((7, channels), BF16),
            vmem((groups, L), F32),
            wide,
            vmem((16, channels), F32),
            vmem((2, 16, channels), BF16),
            vmem((16, channels), BF16),
            wide,
            wide,
            wide,
            vmem((2, 16, half), BF16),
            vmem((2, 16, half), BF16),
            vmem((4, 2, 16, quarter), BF16),
            vmem((2, 16, quarter), BF16),
            vmem((16, 16, L), BF16),
            vmem((16, 16, L), BF16),
            vmem((16, 16, L), BF16),
            vmem((4, 2, 16, quarter), BF16),
            vmem((4, 2, 16, quarter), BF16),
            vmem((2, 16, half), BF16),
            vmem((2, 16, channels), BF16),
            vmem((8, channels), BF16),
            vmem((8, channels), BF16),
            vmem((16, channels), F32),
            vmem((UNROLL, L + 8, L), F32),
            vmem((UNROLL, 24, L), F32),
            dma((3,)), dma((3, SPLIT)), dma((2, 5)), dma((5,)), dma((2, 1)), dma((2, 1)), dma((2, 3)), dma((2, 15)),
            dma((2, 15)), dma((2, 3)), dma((2, 1)), dma((2, SPLIT)), dma((2, SPLIT)),
        ],
        compiler_params=pltpu.CompilerParams(
            collective_id=0, has_side_effects=True, vmem_limit_bytes=58 * 2**20
        ),
    )(
        x,
        gate,
        og,
        decay_rates.T,
        residues.T,
        direct_term.reshape(rows, L),
        short_filter,
        medium_filter,
    )


def solution(mesh):
    placed = (
        P(("ctx", "ch"), None),
        P(("ctx", "ch"), None),
        P(("ctx", "ch"), None),
        P(None, "ch"),
        P(None, "ch"),
        P("ch", None),
        P("ch", None),
        P("ch"),
    )
    return jax.shard_map(
        on_device,
        mesh=mesh,
        in_specs=placed,
        out_specs=(P(("ctx", "ch"), None), P(("ctx", "ch"), None)),
        check_vma=False,
    )
```
